256 devices in a mesh: expert: 32 (over z, x), tensor: 8 (over y, core).
Axes of the slice: x: 4, y: 4, z: 8, core: 2. Of those that a mesh axis runs over, the one named last changes fastest.
Arguments:
- query_latent: bfloat16 [1024, 64, 576], P(('expert', 'tensor')), may hold values from -9 to 9
- kv_cache: bfloat16 [1024, 768, 576], P(('expert', 'tensor')), may hold values from -4 to 4
- cache_len: int32 [1024], P(('expert', 'tensor')), may hold values from 192 to 768, as said below
- value_up: bfloat16 [64, 512, 128], P('tensor'), may hold values from -0.25 to 0.25
- hidden_in: bfloat16 [1024, 7168], P('expert', 'tensor'), may hold values from -6 to 6
- norm_gain: bfloat16 [7168], P('tensor'), may hold values from 0.099609375 to 1.8984375
- expert_ids: int32 [1024, 8], P('expert'), may hold values from 0 to 29, all different within a row; in each aligned block of 32 rows (0 to 31, 32 to 63, ...) at most 18 rows name the same one
- route_weight: int32 [1024, 8], P('expert'), may hold values from 1 to 4095
- placement_plan: int32 [32], replicated, may hold values from 0 to 29, as said below
- updated_list: int32 [30], replicated, may hold values from 0 to 29, each once
- learner_gate: bfloat16 [30, 7168, 1024], P(None, 'expert', 'tensor'), may hold values from -0.0625 to 0.0625
- learner_up: bfloat16 [30, 7168, 1024], P(None, 'expert', 'tensor'), may hold values from -0.0625 to 0.0625
- learner_down: bfloat16 [30, 7168, 1024], P(None, 'expert', 'tensor'), may hold values from -0.1875 to 0.1875
Outputs:
- attn_values: bfloat16 [1024, 8192], P('expert', 'tensor')
- moe_out: bfloat16 [1024, 7168], P('expert', 'tensor')
- slot_gate: bfloat16 [32, 7168, 1024], P('expert', None, 'tensor')
The draws below stay inside these ranges and needn't reach their ends.
Inputs may be any that keep to these rules, and one draw needn't show every extreme that they name: `cache_len`: some row has all 768 positions valid. `placement_plan`: every expert is held by one or two slots; 2 experts by two. `expert_ids`: each row names 8 different experts; among the 32 rows of one device no expert is named more than 18 times. `updated_list`: each expert once.
All inputs are finite; a program needn't handle non-finite values.
Results may differ from the reference program's by a relative error of at most 0.015.
Values may be sent and summed in bfloat16 or wider, within the bound.
No kernel may reach another device: no remote copies, remote signals or barrier semaphores. Data moves between devices by JAX's collectives and lax.ppermute only.
A program may use at most 128 MiB of HBM per device.

```python
import math
import jax
import jax.numpy as jnp
import numpy as np
from jax import lax

D = 7168
FFN = 1024
HEADS = 64
KVL = 512
VH = 128
TOP = 8
ROWS_DEV = 32
CTX = 768
LAT = 576
REDUNDANT = 2
EXPERTS = 30
ROWS = 1024
MOST = 18
N_EXPERT = 32
N_TENSOR = 8


def joint_attention(key):
    key_query = jax.random.fold_in(key, 11)
    key_cache = jax.random.fold_in(key, 12)
    query = jnp.clip(jax.random.normal(key_query, (ROWS, HEADS, LAT), jnp.float32), -4.0, 4.0)
    cache = jnp.clip(jax.random.normal(key_cache, (ROWS, CTX, LAT), jnp.float32), -4.0, 4.0)
    return (query, cache)


def draw_query_latent(key, part):
    query, cache = joint_attention(key)
    return query.astype(jnp.bfloat16)


def draw_kv_cache(key, part):
    query, cache = joint_attention(key)
    return cache.astype(jnp.bfloat16)


def draw_cache_len(key, part):
    drawn = jax.random.randint(jax.random.fold_in(key, 31), (ROWS,), CTX // 4, CTX + 1, dtype=jnp.int32)
    return drawn.at[0].set(CTX)


def draw_placement_plan(key, part):
    first = jax.random.permutation(jax.random.fold_in(key, 21), EXPERTS)
    extra = jax.random.permutation(jax.random.fold_in(key, 22), EXPERTS)[:REDUNDANT]
    joined = jnp.concatenate([first, extra]).astype(jnp.int32)
    return jax.random.permutation(jax.random.fold_in(key, 23), joined).astype(jnp.int32)


def touch_ends(values, stream_key, smallest, top_value):
    place = [jax.random.randint(jax.random.fold_in(stream_key, axis), (), 0, length) for axis, length in enumerate(values.shape)]
    widest = values.shape.index(max(values.shape))
    beside = place[:widest] + [(place[widest] + 1) % values.shape[widest]] + place[widest + 1:]
    return values.at[tuple(place)].set(smallest).at[tuple(beside)].set(top_value)


def block_levels(stream_key, dims, cuts, low, high):
    loudness, own = 1.0, jax.random.fold_in(stream_key, 6)
    for axis_at, parts in cuts:
        heights = jnp.exp(jax.random.uniform(jax.random.fold_in(own, axis_at), (parts,), jnp.float32, low / len(cuts), high / len(cuts)))
        loudness = loudness * jnp.repeat(heights, dims[axis_at] // parts).reshape([-1 if axis == axis_at else 1 for axis in range(len(dims))])
    return loudness


def deal_out(own_key, own, number, rows, number_of, top, bound, slope):
    sequence = jax.random.permutation(own_key, number_of)
    heavy_load, ordinary = portions_of(number_of, rows * top, bound, slope, True), portions_of(number_of, rows * top, bound, slope, False)
    places = jnp.arange(number_of)

    def named(lengths, rotation):
        used = int((lengths > 0).sum())
        fixed = max(1, used // 4)
        passed = fixed + (places - fixed + rotation * (used - fixed)) % max(1, number_of - fixed)
        return jnp.zeros((number_of,), jnp.int32).at[sequence[jnp.where(places < fixed, places, passed)]].set(jnp.asarray(lengths, jnp.int32))

    lengths = jnp.where(number % 4 == 0, named(heavy_load, number // 4), named(ordinary, number - number // 4 - 1))
    mixed = jax.random.permutation(jax.random.fold_in(own, 3), number_of)
    source_of, taker = mixed[0:number_of // 2 * 2:2], mixed[1:number_of // 2 * 2:2]
    slack = jnp.minimum(lengths[source_of] - 1, bound - lengths[taker]) // 2
    slack = jnp.where((source_of == sequence[0]) | (taker == sequence[0]) | (lengths[taker] == 0), 0, jnp.maximum(slack, 0))
    passed = jax.random.randint(jax.random.fold_in(own, 4), (number_of // 2,), 0, 1 << 20) % (slack + 1)
    lengths = lengths.at[source_of].add(-passed).at[taker].add(passed)
    items = jnp.searchsorted(jnp.cumsum(lengths), jnp.arange(rows * top), side="right").astype(jnp.int32)
    table = items.reshape(top, rows).T
    table = table[jax.random.permutation(jax.random.fold_in(own, 1), rows)]
    rotation = jax.random.randint(jax.random.fold_in(own, 2), (rows, 1), 0, top)
    return jnp.take_along_axis(table, (jnp.arange(top)[None, :] + rotation) % top, axis=1)


def portions_of(number_of, total, limit, slope, full):
    portions = [(1 << 20) // math.isqrt(standing ** slope) + 1 for standing in range(1, number_of + 1)]
    largest = limit if full else min(limit, max(-(-total // number_of), total * portions[0] // sum(portions)))
    least = 1 if total - largest >= number_of - 1 else 0
    holding, spare = [largest] + [least] * (number_of - 1), total - largest - least * (number_of - 1)
    while spare > 0:
        movable = [i for i in range(1, number_of) if holding[i] < largest] or [i for i in range(1, number_of) if holding[i] < limit]
        whole, budget = sum([portions[i] for i in movable]), spare
        for i in movable:
            more = min(limit - holding[i], max(1, budget * portions[i] // whole), spare)
            holding[i] = holding[i] + more
            spare = spare - more
    return np.array(holding)


def gaussian(stream_key, extent, width, reach, pieces=(), kind=jnp.bfloat16):
    result = width * jax.random.normal(stream_key, extent, jnp.float32)
    if pieces:
        result = result * block_levels(stream_key, extent, pieces, -0.22, 0.18)
    return jnp.clip(result, -reach, reach).astype(kind)


def setup_inputs(seed: int = 0) -> dict:
    seeds = jax.random.split(jax.random.key(seed), 14)
    query_latent = draw_query_latent(jax.random.fold_in(seeds[13], 71), 0)
    kv_cache = draw_kv_cache(jax.random.fold_in(seeds[13], 71), 0)
    cache_len = draw_cache_len(jax.random.fold_in(seeds[13], 71), 0)
    value_up = gaussian(seeds[3], (HEADS, KVL, VH), KVL ** -0.5, 0.25, ((0, 8),))
    hidden_in = gaussian(seeds[4], (ROWS, D), 1.0, 6.0, ((0, 32), (1, 8)))
    norm_gain = jnp.clip(1.0 + 0.18 * jax.random.normal(seeds[5], (D,), jnp.float32), 0.099609375, 1.8984375).astype(jnp.bfloat16)
    expert_ids_keys = jax.random.split(jax.random.fold_in(seeds[6], 1), ROWS // ROWS_DEV)
    expert_ids_turns = jax.random.permutation(jax.random.fold_in(seeds[6], 3), ROWS // ROWS_DEV)
    expert_ids = jax.vmap(lambda own, number: deal_out(jax.random.fold_in(seeds[6], 2), own, number, ROWS_DEV, EXPERTS, TOP, MOST, 2))(expert_ids_keys, expert_ids_turns).reshape((ROWS, TOP))
    route_weight = touch_ends(jax.random.randint(seeds[7], (ROWS, TOP), 1, 4096), jax.random.fold_in(seeds[7], 1), 1, 4095).astype(jnp.int32)
    placement_plan = draw_placement_plan(jax.random.fold_in(seeds[13], 71), 0)
    updated_list = jax.random.permutation(seeds[9], EXPERTS).astype(jnp.int32)
    learner_gate = gaussian(seeds[10], (EXPERTS, D, FFN), D ** -0.5, 0.0625, ((1, 32), (2, 8)))
    learner_up = gaussian(seeds[11], (EXPERTS, D, FFN), D ** -0.5, 0.0625, ((1, 32), (2, 8)))
    learner_down = gaussian(seeds[12], (EXPERTS, D, FFN), FFN ** -0.5, 0.1875, ((1, 32), (2, 8)))
    return dict(query_latent=query_latent, kv_cache=kv_cache, cache_len=cache_len, value_up=value_up, hidden_in=hidden_in, norm_gain=norm_gain, expert_ids=expert_ids, route_weight=route_weight, placement_plan=placement_plan, updated_list=updated_list, learner_gate=learner_gate, learner_up=learner_up, learner_down=learner_down)


SCORE_SCALE = 192.0 ** (-0.5)
ROUTE_SCALE = 2.5
NORM_EPSILON = 1e-06

def attend(query_latent, kv_cache, cache_len):
    scores = jnp.einsum('rhc,rpc->rhp', query_latent.astype(jnp.float32), kv_cache.astype(jnp.float32)) * SCORE_SCALE
    allowed = (jnp.arange(kv_cache.shape[1], dtype=jnp.int32)[None, :] < cache_len[:, None])[:, None, :]
    scores = jnp.where(allowed, scores, -1e+30)
    highest = lax.optimization_barrier(jnp.max(scores, axis=2, keepdims=True))
    lifted = jnp.where(allowed, jnp.exp(scores - highest), 0.0)
    totals = lax.optimization_barrier(jnp.sum(lifted, axis=2, keepdims=True))
    probs = lifted.astype(jnp.bfloat16).astype(jnp.float32)
    mixed = jnp.einsum('rhp,rpc->rhc', probs, kv_cache[:, :, :KVL].astype(jnp.float32))
    return (mixed / totals).astype(jnp.bfloat16)

def reference(query_latent, kv_cache, cache_len, value_up, hidden_in, norm_gain, expert_ids, route_weight, placement_plan, updated_list, learner_gate, learner_up, learner_down):
    block_rows = ROWS_DEV
    block_count = ROWS // block_rows

    def attend_block(block):
        query_block, cache_block, length_block = block
        latent = attend(query_block, cache_block, length_block)
        values = jnp.einsum('rhc,hcv->rhv', latent.astype(jnp.float32), value_up.astype(jnp.float32))
        return values.astype(jnp.bfloat16).reshape(block_rows, HEADS * VH)
    attn_values = lax.map(attend_block, (query_latent.reshape(block_count, block_rows, HEADS, LAT), kv_cache.reshape(block_count, block_rows, CTX, LAT), cache_len.reshape(block_count, block_rows))).reshape(ROWS, HEADS * VH)
    widened = hidden_in.astype(jnp.float32)
    normed = (widened * lax.rsqrt(lax.optimization_barrier(jnp.mean(widened * widened, axis=1, keepdims=True)) + NORM_EPSILON) * norm_gain.astype(jnp.float32)[None, :]).astype(jnp.bfloat16)
    expert_range = jnp.arange(EXPERTS, dtype=jnp.int32)
    source = lax.optimization_barrier(jnp.sum(expert_range[None, :] * (updated_list[None, :] == expert_range[:, None]).astype(jnp.int32), axis=1)).astype(jnp.int32)
    slot_gate = learner_gate[source[placement_plan]]
    entry_total = ROWS * TOP
    flat_ids = expert_ids.reshape(entry_total)
    buffer_rows = N_EXPERT * MOST
    block_width = FFN // N_TENSOR

    def one_expert(carry, expert):
        members = jnp.nonzero(flat_ids == expert, size=buffer_rows, fill_value=entry_total)[0].astype(jnp.int32)
        alive = members < entry_total
        chosen = normed[jnp.where(alive, members, 0) // TOP]
        entry = source[expert]
        gate_proj = jnp.dot(chosen, learner_gate[entry], preferred_element_type=jnp.float32)
        up_proj = jnp.dot(chosen, learner_up[entry], preferred_element_type=jnp.float32)
        activated = (jax.nn.silu(gate_proj) * up_proj).astype(jnp.bfloat16)
        blocks = jnp.einsum('rbh,dbh->rbd', activated.reshape(buffer_rows, N_TENSOR, block_width).astype(jnp.float32), learner_down[entry].reshape(D, N_TENSOR, block_width).astype(jnp.float32))
        rounded = blocks.astype(jnp.bfloat16).astype(jnp.float32)
        expert_out = lax.optimization_barrier(jnp.sum(rounded, axis=1)).astype(jnp.bfloat16)
        return (carry.at[members].set(expert_out, mode='drop'), None)
    entry_out, ignored = lax.scan(one_expert, jnp.zeros((entry_total, D), jnp.bfloat16), expert_range)
    weights_float = route_weight.astype(jnp.float32)
    gates = ROUTE_SCALE * weights_float / lax.optimization_barrier(jnp.sum(weights_float, axis=1, keepdims=True))
    moe_out = lax.optimization_barrier(jnp.sum(gates[:, :, None] * entry_out.reshape(ROWS, TOP, D).astype(jnp.float32), axis=1)).astype(jnp.bfloat16)
    return (attn_values, moe_out, slot_gate)
```

```python
import jax
import jax.numpy as jnp
from jax import lax
from jax.experimental import pallas as pl
from jax.experimental.pallas import tpu as pltpu
from jax.sharding import PartitionSpec as P

KVL = 512
SCORE_SCALE = 192.0 ** (-0.5)
ROUTE_SCALE = 2.5
NORM_EPSILON = 1e-06

NZ, NX, NT = 8, 4, 8
RB = 32
ZR = NX * RB
ROWS = NZ * ZR
SLICE = 224
WIDE = NX * SLICE
GL = 256
FT = 128
FX = FT // NX
NE = 30
TOP = 8
DIM = 7168

X_GROUPS = [[z * NX + x for x in range(NX)] for z in range(NZ)]
Z_GROUPS = [[z * NX + x for z in range(NZ)] for x in range(NX)]
SWAP = [
    ((z * NX + x) * NT + t, (t * NX + x) * NT + z)
    for z in range(NZ)
    for x in range(NX)
    for t in range(NT)
]
BF = jnp.bfloat16
F32 = jnp.float32


def swap_zt(value):
    return lax.ppermute(value, ("expert", "tensor"), SWAP)


def exchange(value, axis, groups=None):
    return lax.all_to_all(
        value, axis, split_axis=0, concat_axis=0, tiled=True, axis_index_groups=groups
    )


def attend(query_latent, kv_cache, cache_len):
    scores = (
        jnp.einsum("rhc,rpc->rhp", query_latent, kv_cache, preferred_element_type=F32)
        * SCORE_SCALE
    )
    allowed = (jnp.arange(kv_cache.shape[1], dtype=jnp.int32)[None, :] < cache_len[:, None])[
        :, None, :
    ]
    scores = jnp.where(allowed, scores, -1e30)
    highest = jnp.max(scores, axis=2, keepdims=True)
    lifted = jnp.where(allowed, jnp.exp(scores - highest), 0.0)
    totals = jnp.sum(lifted, axis=2, keepdims=True)
    mixed = jnp.einsum(
        "rhp,rpc->rhc",
        lifted.astype(BF),
        kv_cache[:, :, :KVL],
        preferred_element_type=F32,
    )
    return (mixed / totals).astype(BF)


def iota(shape, axis):
    return lax.broadcasted_iota(jnp.int32, shape, axis)


def flip(block):
    turned = jnp.transpose(block.astype(F32))
    return jnp.concatenate([turned, jnp.zeros((FT, GL - SLICE), F32)], axis=1).astype(BF)


def gate_up_body(g_ref, u_ref, o_ref):
    for e in range(g_ref.shape[0]):
        g = flip(g_ref[e])
        u = flip(u_ref[e])
        for x in range(NX):
            o_ref[x, e, 0:FX, :] = g[x * FX : (x + 1) * FX]
            o_ref[x, e, FX : 2 * FX, :] = u[x * FX : (x + 1) * FX]


def down_body(d_ref, o_ref):
    for e in range(d_ref.shape[0]):
        d = flip(d_ref[e])
        for x in range(NX):
            o_ref[x, e] = d[x * FX : (x + 1) * FX]


STEP_E = 5


def turn_gate_up(gate, up):
    spec = pl.BlockSpec((STEP_E, SLICE, FT), lambda i: (i, 0, 0))
    return pl.pallas_call(
        gate_up_body,
        grid=(NE // STEP_E,),
        in_specs=[spec, spec],
        out_specs=pl.BlockSpec((NX, STEP_E, 2 * FX, GL), lambda i: (0, i, 0, 0)),
        out_shape=jax.ShapeDtypeStruct((NX, NE, 2 * FX, GL), BF),
        name="turn_gate_up",
    )(gate, up)


def turn_down(down):
    return pl.pallas_call(
        down_body,
        grid=(NE // STEP_E,),
        in_specs=[pl.BlockSpec((STEP_E, SLICE, FT), lambda i: (i, 0, 0))],
        out_specs=pl.BlockSpec((NX, STEP_E, FX, GL), lambda i: (0, i, 0, 0)),
        out_shape=jax.ShapeDtypeStruct((NX, NE, FX, GL), BF),
        name="turn_down",
    )(down)


META = 96
HIGH, LOW, SQ = META + 8, META + 16, META + 24
PR = 4 * ZR
PB = PR + 16


def project_body(x_ref, w_ref, p_ref, id_ref, y_ref):
    meta = x_ref[:, 128:256]
    col = iota((128, TOP * 128), 1)
    pick = (iota((128, TOP * 128), 0) - META == col // 128).astype(F32).astype(BF)
    spread = jnp.dot(meta, pick, preferred_element_type=F32)
    half = (iota((1, TOP * 128), 1) % 128 // 64).astype(F32)
    id_ref[...] = (spread - half).astype(BF)
    for start in range(0, NE * 2 * FX, 256):
        size = min(256, NE * 2 * FX - start)
        total = None
        for k in range(NX):
            part = lax.dot_general(
                x_ref[:, k * GL : (k + 1) * GL],
                w_ref[k, start : start + size, :],
                (((1,), (1,)), ((), ())),
                preferred_element_type=F32,
            )
            total = part if total is None else total + part
        y_ref[:, start : start + size] = total.astype(BF)
    low_half = iota((16, 128), 1) < 64

    def body(s, carry):
        r = pl.multiple_of(s * 16, 16)
        z = s // 8
        rr = pl.multiple_of((s % 8) * 16, 16)
        ids = [id_ref[pl.ds(r, 16), j * 128 : (j + 1) * 128] for j in range(TOP)]
        kept = [jnp.zeros((16, 128), BF) for _ in range(TOP)]
        for tile in range(NE // 2):
            y = y_ref[pl.ds(r, 16), tile * 128 : (tile + 1) * 128]
            for j in range(TOP):
                kept[j] = jnp.where(ids[j] == jnp.asarray(2.0 * tile, BF), y, kept[j])
        for q in range(TOP // 2):
            a = kept[2 * q].astype(F32)
            b = kept[2 * q + 1].astype(F32)
            a = a + pltpu.roll(a, 64, 1)
            b = b + pltpu.roll(b, 64, 1)
            p_ref[z, pl.ds(q * ZR + rr, 16), :] = jnp.where(low_half, a, b).astype(BF)
        return carry

    lax.fori_loop(0, ROWS // 16, body, 0)
    for z in range(NZ):
        turned = jnp.transpose(x_ref[z * ZR : (z + 1) * ZR, 128:256].astype(F32))
        p_ref[z, PR:PB, :] = turned[112:128].astype(BF)


def project(rows, weights):
    return pl.pallas_call(
        project_body,
        out_shape=jax.ShapeDtypeStruct((NZ, PB, 128), BF),
        scratch_shapes=[
            pltpu.VMEM((ROWS, TOP * 128), BF),
            pltpu.VMEM((ROWS, NE * 2 * FX), BF),
        ],
        name="project",
    )(rows, weights)


def activate_body(p_ref, m_ref, o_ref):
    row = iota((128, 5 * 128), 0)
    col = iota((128, 5 * 128), 1)
    j = 2 * (col // 128) + (col % 128) // 64
    single = jnp.where(row == HIGH + j, 64.0, jnp.where(row == LOW + j, 1.0, 0.0))
    every = jnp.where(
        (row >= HIGH) & (row < LOW), 64.0, jnp.where((row >= LOW) & (row < SQ), 1.0, 0.0)
    )
    pick = jnp.where(col < 512, single, every).astype(BF)
    weights = jnp.dot(m_ref[...], pick, preferred_element_type=F32)
    scale = ROUTE_SCALE / weights[:, 512:640]
    squares = jnp.zeros((16, 128), F32)
    for z in range(NZ):
        squares = squares + p_ref[z, PR:PB, :].astype(F32)
    total = squares[8:9] + squares[9:10]
    inv = lax.rsqrt(total * (1.0 / DIM) + NORM_EPSILON)
    inv = jnp.transpose(jnp.broadcast_to(inv, (128, 128)))
    acts = []
    for q in range(TOP // 2):
        v = jnp.zeros((ZR, 128), F32)
        for z in range(NZ):
            v = v + p_ref[z, q * ZR : (q + 1) * ZR, :].astype(F32)
        v = v * inv
        u = pltpu.roll(v, 128 - FX, 1)
        gate = weights[:, q * 128 : (q + 1) * 128] * scale
        acts.append(v / (1.0 + jnp.exp(-v)) * u * gate)
    first = iota((ZR, 128), 1) % 64 < FX
    for q in range(2):
        packed = jnp.where(first, acts[2 * q], pltpu.roll(acts[2 * q + 1], FX, 1)).astype(BF)
        for z in range(NZ):
            o_ref[z, q * ZR : (q + 1) * ZR, :] = packed


def activate(parts, meta):
    return pl.pallas_call(
        activate_body,
        out_shape=jax.ShapeDtypeStruct((NZ, 2 * ZR, 128), BF),
        name="activate",
    )(parts, meta)


def combine_body(a_ref, x_ref, d_ref, o_ref, id_ref, wide_ref):
    meta = x_ref[:, 128:256]
    row = iota((128, TOP * 128), 0) - META
    col = iota((128, TOP * 128), 1)
    q = col // 512
    k = col // 128 % 4
    block = col % 128 // FX
    origin = (block - k + 4) % 4
    j = 4 * q + jnp.where(origin == 1, 2, jnp.where(origin == 2, 1, origin))
    spread = jnp.dot(meta, (row == j).astype(F32).astype(BF), preferred_element_type=F32)
    id_ref[...] = (spread - (iota((1, TOP * 128), 1) % 128 // FX).astype(F32)).astype(BF)

    def body(s, carry):
        r = pl.multiple_of(s * 16, 16)
        z = s // 8
        rr = pl.multiple_of((s % 8) * 16, 16)
        ids = [id_ref[pl.ds(r, 16), n * 128 : (n + 1) * 128] for n in range(TOP)]
        turned = []
        for n in range(2):
            a = a_ref[z, pl.ds(n * ZR + rr, 16), :].astype(F32)
            for shift in range(4):
                moved = a if shift == 0 else pltpu.roll(a, shift * FX, 1)
                turned.append(moved.astype(BF))
        for g in range(8):
            kept = jnp.zeros((16, 128), BF)
            for n in range(TOP):
                kept = jnp.where(ids[n] == jnp.asarray(4.0 * g, BF), turned[n], kept)
            wide_ref[pl.ds(r, 16), g * 128 : (g + 1) * 128] = kept
        return carry

    lax.fori_loop(0, ROWS // 16, body, 0)
    for x in range(NX):
        out = lax.dot_general(
            wide_ref[:, : NE * FX],
            d_ref[x],
            (((1,), (0,)), ((), ())),
            preferred_element_type=F32,
        )
        o_ref[:, x * SLICE : (x + 1) * SLICE] = out[:, :SLICE].astype(BF)


def combine(acts, rows, down):
    return pl.pallas_call(
        combine_body,
        out_shape=jax.ShapeDtypeStruct((ROWS, WIDE), BF),
        scratch_shapes=[
            pltpu.VMEM((ROWS, TOP * 128), BF),
            pltpu.VMEM((ROWS, 1024), BF),
        ],
        name="combine",
    )(acts, rows, down)


def pack_rows(hidden_in, norm_gain, expert_ids, route_weight, updated_list):
    named = updated_list[None, None, :] == expert_ids[:, :, None]
    entries = jnp.sum(
        jnp.where(named, jnp.arange(NE, dtype=jnp.int32)[None, None, :], 0), axis=2
    )
    widened = hidden_in.astype(F32)
    scaled = (widened * norm_gain.astype(F32)[None, :]).astype(BF)
    squares = jnp.sum(widened * widened, axis=1, keepdims=True)
    high = lax.reduce_precision(squares, 8, 7)
    meta = jnp.concatenate(
        [
            entries.astype(F32),
            (route_weight // 64).astype(F32),
            (route_weight % 64).astype(F32),
            high,
            squares - high,
            jnp.zeros((RB, GL - SLICE - 26), F32),
        ],
        axis=1,
    ).astype(BF)
    pad = jnp.zeros((RB, GL - SLICE), BF)
    pieces = []
    for k in range(NX):
        pieces += [scaled[:, k * SLICE : (k + 1) * SLICE], meta if k == 0 else pad]
    return jnp.concatenate(pieces, axis=1)


def gather_rows(packed):
    moved = swap_zt(packed)
    copies = [moved] + [
        lax.ppermute(
            moved,
            "expert",
            [(z * NX + x, z * NX + (x + s) % NX) for z in range(NZ) for x in range(NX)],
        )
        for s in range(1, NX)
    ]
    own = lax.axis_index("expert") % NX
    stacked = jnp.concatenate(copies, axis=0)
    order = (own - jnp.arange(NX, dtype=jnp.int32)) % NX
    ring = jnp.take(
        stacked.reshape(NX, RB, stacked.shape[1]), order, axis=0, mode="clip"
    ).reshape(ZR, stacked.shape[1])
    spread = exchange(jnp.broadcast_to(ring[None], (NT,) + ring.shape), "tensor")
    return spread.reshape(ROWS, spread.shape[2])


def per_device(
    query_latent,
    kv_cache,
    cache_len,
    value_up,
    hidden_in,
    norm_gain,
    expert_ids,
    route_weight,
    placement_plan,
    updated_list,
    learner_gate,
    learner_up,
    learner_down,
):
    turned = turn_gate_up(learner_gate, learner_up)
    held = exchange(turned.reshape(NX, NE * 2 * FX, GL), "expert", X_GROUPS)
    rows = gather_rows(pack_rows(hidden_in, norm_gain, expert_ids, route_weight, updated_list))
    held_down = exchange(
        turn_down(learner_down).reshape(NX, NE * FX, GL), "expert", X_GROUPS
    )
    parts = exchange(project(rows, held), "expert", Z_GROUPS)
    z = lax.axis_index("expert") // NX
    meta = lax.dynamic_slice(rows, (z * ZR, 128), (ZR, 128))
    acts = exchange(activate(parts, meta), "expert", Z_GROUPS)

    entry_range = jnp.arange(NE, dtype=jnp.int32)
    learner_entry = jnp.sum(
        entry_range[None, :] * (updated_list[None, :] == placement_plan[:, None]).astype(jnp.int32),
        axis=1,
    )
    chosen = jnp.take(learner_gate, learner_entry, axis=0, mode="clip")
    slot_gate = lax.all_to_all(chosen, "expert", split_axis=0, concat_axis=1, tiled=True)

    partial = combine(acts, rows, held_down)
    shared = exchange(partial.reshape(NT, ZR, WIDE), "tensor")
    summed = jnp.sum(shared.astype(F32), axis=0).astype(BF)
    crossed = exchange(summed.reshape(NX, RB, WIDE), "expert", X_GROUPS)
    moe_out = swap_zt(jnp.sum(crossed.astype(F32), axis=0).astype(BF))

    latent = attend(query_latent, kv_cache, cache_len)
    head_rows = lax.all_to_all(latent, "tensor", split_axis=1, concat_axis=0, tiled=True)
    projected = jnp.einsum("rhc,hcv->rhv", head_rows, value_up, preferred_element_type=F32)
    attn_values = projected.astype(BF).reshape(
        head_rows.shape[0], projected.shape[1] * projected.shape[2]
    )
    return (attn_values, moe_out, slot_gate)


def solution(mesh):
    in_specs = (
        P(("expert", "tensor"), None, None),
        P(("expert", "tensor"), None, None),
        P(("expert", "tensor")),
        P("tensor", None, None),
        P("expert", "tensor"),
        P("tensor"),
        P("expert", None),
        P("expert", None),
        P(),
        P(),
        P(None, "expert", "tensor"),
        P(None, "expert", "tensor"),
        P(None, "expert", "tensor"),
    )
    out_specs = (P("expert", "tensor"), P("expert", "tensor"), P("expert", None, "tensor"))
    return jax.shard_map(
        per_device, mesh=mesh, in_specs=in_specs, out_specs=out_specs, check_vma=False
    )
```

```python
import jax
import jax.numpy as jnp
from jax import lax
from jax.experimental import pallas as pl
from jax.experimental.pallas import tpu as pltpu
from jax.sharding import PartitionSpec as P


KVL = 512
SCORE_SCALE = 192.0 ** (-0.5)
ROUTE_SCALE = 2.5
NORM_EPSILON = 1e-06

NZ, NX, NT, NY = 8, 4, 8, 4
RB = 32
ZR = NX * RB
ROWS = NZ * ZR
SLICE = 224
WIDE = NX * SLICE
GL = 256
FT = 128
FX = FT // NX
NE = 30
TOP = 8
DIM = 7168

X_GROUPS = [[z * NX + x for x in range(NX)] for z in range(NZ)]
Z_GROUPS = [[z * NX + x for z in range(NZ)] for x in range(NX)]
SWAP = [
    ((z * NX + x) * NT + t, (t * NX + x) * NT + z)
    for z in range(NZ)
    for x in range(NX)
    for t in range(NT)
]
BF = jnp.bfloat16
F32 = jnp.float32


def swap_zt(value):
    return lax.ppermute(value, ("expert", "tensor"), SWAP)


def exchange(value, groups):
    return lax.all_to_all(
        value, "expert", split_axis=0, concat_axis=0, tiled=True, axis_index_groups=groups
    )


def shift_x(value, step):
    pairs = [(z * NX + x, z * NX + (x + step) % NX) for z in range(NZ) for x in range(NX)]
    return lax.ppermute(value, "expert", pairs)


def shift_y(value, step):
    pairs = [(y * 2 + c, (y + step) % NY * 2 + c) for y in range(NY) for c in range(2)]
    return lax.ppermute(value, "tensor", pairs)


def other_core(value):
    return lax.ppermute(value, "tensor", [(t, t ^ 1) for t in range(NT)])


def attend(query_latent, kv_cache, cache_len):
    scores = (
        jnp.einsum("rhc,rpc->rhp", query_latent, kv_cache, preferred_element_type=F32)
        * SCORE_SCALE
    )
    allowed = (jnp.arange(kv_cache.shape[1], dtype=jnp.int32)[None, :] < cache_len[:, None])[
        :, None, :
    ]
    scores = jnp.where(allowed, scores, -1e30)
    highest = jnp.max(scores, axis=2, keepdims=True)
    lifted = jnp.where(allowed, jnp.exp(scores - highest), 0.0)
    totals = jnp.sum(lifted, axis=2, keepdims=True)
    mixed = jnp.einsum(
        "rhp,rpc->rhc",
        lifted.astype(BF),
        kv_cache[:, :, :KVL],
        preferred_element_type=F32,
    )
    return (mixed / totals).astype(BF)


def iota(shape, axis):
    return lax.broadcasted_iota(jnp.int32, shape, axis)


def flip(block):
    turned = jnp.transpose(block.astype(F32))
    return jnp.concatenate([turned, jnp.zeros((FT, GL - SLICE), F32)], axis=1).astype(BF)


def gate_up_body(g_ref, u_ref, o_ref):
    for e in range(g_ref.shape[0]):
        g = flip(g_ref[e])
        u = flip(u_ref[e])
        for x in range(NX):
            o_ref[x, e, 0:FX, :] = g[x * FX : (x + 1) * FX]
            o_ref[x, e, FX : 2 * FX, :] = u[x * FX : (x + 1) * FX]


def down_body(d_ref, o_ref):
    for e in range(d_ref.shape[0]):
        d = flip(d_ref[e])
        for x in range(NX):
            o_ref[x, e] = d[x * FX : (x + 1) * FX]


STEP_E = 5


def turn_gate_up(gate, up):
    spec = pl.BlockSpec((STEP_E, SLICE, FT), lambda i: (i, 0, 0))
    return pl.pallas_call(
        gate_up_body,
        grid=(NE // STEP_E,),
        in_specs=[spec, spec],
        out_specs=pl.BlockSpec((NX, STEP_E, 2 * FX, GL), lambda i: (0, i, 0, 0)),
        out_shape=jax.ShapeDtypeStruct((NX, NE, 2 * FX, GL), BF),
        compiler_params=pltpu.CompilerParams(vmem_limit_bytes=16 << 20),
        name="turn_gate_up",
    )(gate, up)


def turn_down(down):
    return pl.pallas_call(
        down_body,
        grid=(NE // STEP_E,),
        in_specs=[pl.BlockSpec((STEP_E, SLICE, FT), lambda i: (i, 0, 0))],
        out_specs=pl.BlockSpec((NX, STEP_E, FX, GL), lambda i: (0, i, 0, 0)),
        out_shape=jax.ShapeDtypeStruct((NX, NE, FX, GL), BF),
        compiler_params=pltpu.CompilerParams(vmem_limit_bytes=16 << 20),
        name="turn_down",
    )(down)


META = 96
HIGH, LOW, SQ = META + 8, META + 16, META + 24
PR = 4 * ZR
PB = PR + 16


def project_body(z_ref, *refs):
    x_refs, (w_ref, p_ref, id_ref, y_ref) = refs[:NZ], refs[NZ:]
    meta = jnp.concatenate([x[:, 128:256] for x in x_refs], axis=0)
    col = iota((128, TOP * 128), 1)
    pick = (iota((128, TOP * 128), 0) - META == col // 128).astype(F32).astype(BF)
    spread = jnp.dot(meta, pick, preferred_element_type=F32)
    half = (iota((1, TOP * 128), 1) % 128 // 64).astype(F32)
    id_ref[...] = (spread - half).astype(BF)
    for start in range(0, NE * 2 * FX, 256):
        size = min(256, NE * 2 * FX - start)
        total = None
        for k in range(NX):
            part = lax.dot_general(
                jnp.concatenate([x[:, k * GL : (k + 1) * GL] for x in x_refs], axis=0),
                w_ref[k, start : start + size, :],
                (((1,), (1,)), ((), ())),
                preferred_element_type=F32,
            )
            total = part if total is None else total + part
        y_ref[:, start : start + size] = total.astype(BF)
    low_half = iota((16, 128), 1) < 64

    def body(s, carry):
        r = pl.multiple_of(s * 16, 16)
        z = z_ref[s // 8]
        rr = pl.multiple_of((s % 8) * 16, 16)
        ids = [id_ref[pl.ds(r, 16), j * 128 : (j + 1) * 128] for j in range(TOP)]
        kept = [jnp.zeros((16, 128), BF) for _ in range(TOP)]
        for tile in range(NE // 2):
            y = y_ref[pl.ds(r, 16), tile * 128 : (tile + 1) * 128]
            for j in range(TOP):
                kept[j] = jnp.where(ids[j] == jnp.asarray(2.0 * tile, BF), y, kept[j])
        for q in range(TOP // 2):
            a = kept[2 * q].astype(F32)
            b = kept[2 * q + 1].astype(F32)
            a = a + pltpu.roll(a, 64, 1)
            b = b + pltpu.roll(b, 64, 1)
            p_ref[z, pl.ds(q * ZR + rr, 16), :] = jnp.where(low_half, a, b).astype(BF)
        return carry

    lax.fori_loop(0, ROWS // 16, body, 0)
    for n in range(NZ):
        turned = jnp.transpose(x_refs[n][:, 128:256].astype(F32))
        p_ref[z_ref[n], PR:PB, :] = turned[112:128].astype(BF)


SMEM = pl.BlockSpec(memory_space=pltpu.SMEM)
VMEM = pl.BlockSpec(memory_space=pltpu.VMEM)


def project(blocks, rows, weights):
    return pl.pallas_call(
        project_body,
        in_specs=[SMEM] + [VMEM] * (NZ + 1),
        out_shape=jax.ShapeDtypeStruct((NZ, PB, 128), BF),
        scratch_shapes=[
            pltpu.VMEM((ROWS, TOP * 128), BF),
            pltpu.VMEM((ROWS, NE * 2 * FX), BF),
        ],
        compiler_params=pltpu.CompilerParams(vmem_limit_bytes=32 << 20),
        name="project",
    )(blocks, *rows, weights)


def activate_body(p_ref, m_ref, o_ref):
    row = iota((128, 5 * 128), 0)
    col = iota((128, 5 * 128), 1)
    j = 2 * (col // 128) + (col % 128) // 64
    single = jnp.where(row == HIGH + j, 64.0, jnp.where(row == LOW + j, 1.0, 0.0))
    every = jnp.where(
        (row >= HIGH) & (row < LOW), 64.0, jnp.where((row >= LOW) & (row < SQ), 1.0, 0.0)
    )
    pick = jnp.where(col < 512, single, every).astype(BF)
    weights = jnp.dot(m_ref[...], pick, preferred_element_type=F32)
    scale = ROUTE_SCALE / weights[:, 512:640]
    squares = jnp.zeros((16, 128), F32)
    for z in range(NZ):
        squares = squares + p_ref[z, PR:PB, :].astype(F32)
    total = squares[8:9] + squares[9:10]
    inv = lax.rsqrt(total * (1.0 / DIM) + NORM_EPSILON)
    inv = jnp.transpose(jnp.broadcast_to(inv, (128, 128)))
    acts = []
    for q in range(TOP // 2):
        v = jnp.zeros((ZR, 128), F32)
        for z in range(NZ):
            v = v + p_ref[z, q * ZR : (q + 1) * ZR, :].astype(F32)
        v = v * inv
        u = pltpu.roll(v, 128 - FX, 1)
        gate = weights[:, q * 128 : (q + 1) * 128] * scale
        acts.append(v / (1.0 + jnp.exp(-v)) * u * gate)
    first = iota((ZR, 128), 1) % 64 < FX
    for q in range(2):
        packed = jnp.where(first, acts[2 * q], pltpu.roll(acts[2 * q + 1], FX, 1)).astype(BF)
        for z in range(NZ):
            o_ref[z, q * ZR : (q + 1) * ZR, :] = packed


def activate(parts, meta):
    return pl.pallas_call(
        activate_body,
        out_shape=jax.ShapeDtypeStruct((NZ, 2 * ZR, 128), BF),
        compiler_params=pltpu.CompilerParams(vmem_limit_bytes=12 << 20),
        name="activate",
    )(parts, meta)


def combine_body(z_ref, a_ref, *refs):
    x_refs, d_refs = refs[:NZ], refs[NZ : NZ + NX]
    near_ref, far_ref, id_ref, wide_ref, d_ref = refs[NZ + NX :]
    for s in range(NX):
        d_ref[(z_ref[NZ] + NX - s) % NX] = d_refs[s][...]
    meta = jnp.concatenate([x[:, 128:256] for x in x_refs], axis=0)
    row = iota((128, TOP * 128), 0) - META
    col = iota((128, TOP * 128), 1)
    q = col // 512
    k = col // 128 % 4
    block = col % 128 // FX
    origin = (block - k + 4) % 4
    j = 4 * q + jnp.where(origin == 1, 2, jnp.where(origin == 2, 1, origin))
    spread = jnp.dot(meta, (row == j).astype(F32).astype(BF), preferred_element_type=F32)
    id_ref[...] = (spread - (iota((1, TOP * 128), 1) % 128 // FX).astype(F32)).astype(BF)

    def body(s, carry):
        r = pl.multiple_of(s * 16, 16)
        z = z_ref[s // 8]
        rr = pl.multiple_of((s % 8) * 16, 16)
        ids = [id_ref[pl.ds(r, 16), n * 128 : (n + 1) * 128] for n in range(TOP)]
        turned = []
        for n in range(2):
            a = a_ref[z, pl.ds(n * ZR + rr, 16), :].astype(F32)
            for shift in range(4):
                moved = a if shift == 0 else pltpu.roll(a, shift * FX, 1)
                turned.append(moved.astype(BF))
        for g in range(8):
            kept = jnp.zeros((16, 128), BF)
            for n in range(TOP):
                kept = jnp.where(ids[n] == jnp.asarray(4.0 * g, BF), turned[n], kept)
            wide_ref[pl.ds(r, 16), g * 128 : (g + 1) * 128] = kept
        return carry

    lax.fori_loop(0, ROWS // 16, body, 0)
    for x in range(NX):
        out = lax.dot_general(
            wide_ref[:, : NE * FX],
            d_ref[x],
            (((1,), (0,)), ((), ())),
            preferred_element_type=F32,
        )
        out = out[:, :SLICE].astype(BF)
        near_ref[:, x * SLICE : (x + 1) * SLICE] = out[: ROWS // 2]
        far_ref[:, x * SLICE : (x + 1) * SLICE] = out[ROWS // 2 :]


def combine(blocks, acts, rows, down):
    return pl.pallas_call(
        combine_body,
        in_specs=[SMEM] + [VMEM] * (NZ + 1 + NX),
        out_specs=[VMEM] * 2,
        out_shape=[jax.ShapeDtypeStruct((ROWS // 2, WIDE), BF)] * 2,
        scratch_shapes=[
            pltpu.VMEM((ROWS, TOP * 128), BF),
            pltpu.VMEM((ROWS, 1024), BF),
            pltpu.VMEM((NX, NE * FX, GL), BF),
        ],
        compiler_params=pltpu.CompilerParams(vmem_limit_bytes=28 << 20),
        name="combine",
    )(blocks, acts, *rows, *down)


def pack_rows(hidden_in, norm_gain, expert_ids, route_weight, updated_list):
    named = updated_list[None, None, :] == expert_ids[:, :, None]
    entries = jnp.sum(
        jnp.where(named, jnp.arange(NE, dtype=jnp.int32)[None, None, :], 0), axis=2
    )
    widened = hidden_in.astype(F32)
    scaled = (widened * norm_gain.astype(F32)[None, :]).astype(BF)
    squares = jnp.sum(widened * widened, axis=1, keepdims=True)
    high = lax.reduce_precision(squares, 8, 7)
    meta = jnp.concatenate(
        [
            entries.astype(F32),
            (route_weight // 64).astype(F32),
            (route_weight % 64).astype(F32),
            high,
            squares - high,
            jnp.zeros((RB, GL - SLICE - 26), F32),
        ],
        axis=1,
    ).astype(BF)
    pad = jnp.zeros((RB, GL - SLICE), BF)
    pieces = []
    for k in range(NX):
        pieces += [scaled[:, k * SLICE : (k + 1) * SLICE], meta if k == 0 else pad]
    return jnp.concatenate(pieces, axis=1)


def gather_rows(packed):
    moved = swap_zt(packed)
    ring = jnp.concatenate([moved] + [shift_x(moved, s) for s in range(1, NX)], axis=0)
    mine = [ring] + [shift_y(ring, s) for s in range(1, NY)]
    return mine + [other_core(block) for block in mine]


def block_places():
    t = lax.axis_index("tensor")
    y, c = t // 2, t % 2
    s = jnp.arange(NY, dtype=jnp.int32)
    turn = (y - s) % NY * 2
    blocks = jnp.concatenate([turn + c, turn + 1 - c]).astype(jnp.int32)
    zs = jnp.arange(NZ, dtype=jnp.int32)
    places = (y - zs // 2) % NY + NY * (zs % 2 != c).astype(jnp.int32)
    return blocks, places.astype(jnp.int32)


def swap_down(down):
    own = lax.axis_index("expert") % NX
    mine = [
        lax.dynamic_index_in_dim(down, (own + s) % NX, 0, keepdims=False) for s in range(NX)
    ]
    return mine[:1] + [shift_x(mine[s], s) for s in range(1, NX)]


def add(values):
    total = values[0].astype(F32)
    for value in values[1:]:
        total = total + value.astype(F32)
    return total.astype(BF)


def gather_out(near, far):
    size = near.shape[0] // NY
    blocks = [
        add([near[s * size : (s + 1) * size], far[s * size : (s + 1) * size]]) for s in range(NY)
    ]
    came = [blocks[0]] + [shift_y(blocks[s], NY - s) for s in range(1, NY)]
    pieces = [add([b[s * RB : (s + 1) * RB] for b in came]) for s in range(NX)]
    came = [pieces[0]] + [shift_x(pieces[s], NX - s) for s in range(1, NX)]
    return swap_zt(add(came))


def device_body(
    query_latent,
    kv_cache,
    cache_len,
    value_up,
    hidden_in,
    norm_gain,
    expert_ids,
    route_weight,
    placement_plan,
    updated_list,
    learner_gate,
    learner_up,
    learner_down,
):
    turned = turn_gate_up(learner_gate, learner_up)
    held = exchange(turned.reshape(NX, NE * 2 * FX, GL), X_GROUPS)
    rows = gather_rows(pack_rows(hidden_in, norm_gain, expert_ids, route_weight, updated_list))
    blocks, places = block_places()
    down = turn_down(learner_down).reshape(NX, NE * FX, GL)
    held_down = swap_down(down)
    parts = exchange(project(blocks, rows, held), Z_GROUPS)
    z = lax.axis_index("expert") // NX
    place = places[z]
    metas = jnp.stack([block[:, 128:256] for block in rows])
    meta = lax.dynamic_index_in_dim(metas, place, 0, keepdims=False)
    acts = exchange(activate(parts, meta), Z_GROUPS)

    entry_range = jnp.arange(NE, dtype=jnp.int32)
    learner_entry = jnp.sum(
        entry_range[None, :] * (updated_list[None, :] == placement_plan[:, None]).astype(jnp.int32),
        axis=1,
    )
    chosen = jnp.take(learner_gate, learner_entry, axis=0, mode="clip")
    slot_gate = lax.all_to_all(chosen, "expert", split_axis=0, concat_axis=1, tiled=True)

    near, far = combine(
        jnp.concatenate([blocks, lax.axis_index("expert").astype(jnp.int32)[None] % NX]),
        acts,
        rows,
        held_down,
    )
    far = other_core(far)
    moe_out = gather_out(near, far)

    latent = attend(query_latent, kv_cache, cache_len)
    head_rows = lax.all_to_all(latent, "tensor", split_axis=1, concat_axis=0, tiled=True)
    projected = jnp.einsum("rhc,hcv->rhv", head_rows, value_up, preferred_element_type=F32)
    attn_values = projected.astype(BF).reshape(
        head_rows.shape[0], projected.shape[1] * projected.shape[2]
    )
    return (attn_values, moe_out, slot_gate)


def solution(mesh):
    in_specs = (
        P(("expert", "tensor"), None, None),
        P(("expert", "tensor"), None, None),
        P(("expert", "tensor")),
        P("tensor", None, None),
        P("expert", "tensor"),
        P("tensor"),
        P("expert", None),
        P("expert", None),
        P(),
        P(),
        P(None, "expert", "tensor"),
        P(None, "expert", "tensor"),
        P(None, "expert", "tensor"),
    )
    out_specs = (P("expert", "tensor"), P("expert", "tensor"), P("expert", None, "tensor"))
    return jax.shard_map(
        device_body, mesh=mesh, in_specs=in_specs, out_specs=out_specs, check_vma=False
    )
```

```python
import jax
import jax.numpy as jnp
from jax import lax
from jax.experimental import pallas as pl
from jax.experimental.pallas import tpu as pltpu
from jax.sharding import PartitionSpec as P


KVL = 512
SCORE_SCALE = 192.0 ** (-0.5)
ROUTE_SCALE = 2.5
NORM_EPSILON = 1e-06

NZ, NX, NT, NY = 8, 4, 8, 4
RB = 32
ZR = NX * RB
ROWS = NZ * ZR
SLICE = 224
WIDE = NX * SLICE
GL = 256
FT = 128
FX = FT // NX
NE = 30
TOP = 8
DIM = 7168

Z_GROUPS = [[z * NX + x for z in range(NZ)] for x in range(NX)]
SWAP = [
    ((z * NX + x) * NT + t, (t * NX + x) * NT + z)
    for z in range(NZ)
    for x in range(NX)
    for t in range(NT)
]
BF = jnp.bfloat16
F32 = jnp.float32


def swap_zt(value):
    return lax.ppermute(value, ("expert", "tensor"), SWAP)


def exchange(value, groups):
    return lax.all_to_all(
        value, "expert", split_axis=0, concat_axis=0, tiled=True, axis_index_groups=groups
    )


def shift_x(value, step):
    pairs = [(z * NX + x, z * NX + (x + step) % NX) for z in range(NZ) for x in range(NX)]
    return lax.ppermute(value, "expert", pairs)


def shift_y(value, step):
    pairs = [(y * 2 + c, (y + step) % NY * 2 + c) for y in range(NY) for c in range(2)]
    return lax.ppermute(value, "tensor", pairs)


def other_core(value):
    return lax.ppermute(value, "tensor", [(t, t ^ 1) for t in range(NT)])


def attend(query_latent, kv_cache, cache_len):
    scores = (
        jnp.einsum("rhc,rpc->rhp", query_latent, kv_cache, preferred_element_type=F32)
        * SCORE_SCALE
    )
    allowed = (jnp.arange(kv_cache.shape[1], dtype=jnp.int32)[None, :] < cache_len[:, None])[
        :, None, :
    ]
    scores = jnp.where(allowed, scores, -1e30)
    highest = jnp.max(scores, axis=2, keepdims=True)
    lifted = jnp.where(allowed, jnp.exp(scores - highest), 0.0)
    totals = jnp.sum(lifted, axis=2, keepdims=True)
    mixed = jnp.einsum(
        "rhp,rpc->rhc",
        lifted.astype(BF),
        kv_cache[:, :, :KVL],
        preferred_element_type=F32,
    )
    return (mixed / totals).astype(BF)


def iota(shape, axis):
    return lax.broadcasted_iota(jnp.int32, shape, axis)


def flip(block):
    turned = jnp.transpose(block.astype(F32))
    return jnp.concatenate([turned, jnp.zeros((FT, GL - SLICE), F32)], axis=1).astype(BF)


SMEM = pl.BlockSpec(memory_space=pltpu.SMEM)
VMEM = pl.BlockSpec(memory_space=pltpu.VMEM)
HEAD = 16


def gate_up_body(own_ref, g_ref, u_ref, *refs):
    outs, (turn_ref,) = refs[:5], refs[5:]
    own = own_ref[0]

    def turn(e, carry):
        turn_ref[0, e] = flip(g_ref[e])
        turn_ref[1, e] = flip(u_ref[e])
        return carry

    lax.fori_loop(0, NE, turn, 0, unroll=5)
    for s in range(NX):
        at = pl.multiple_of((own + s) % NX * FX, FX)
        spans = [(outs[s], 0, NE)]
        if s == 2:
            spans = [(outs[2], 0, HEAD), (outs[4], HEAD, NE)]
        for out, low, high in spans:

            def copy(e, carry, out=out, low=low, at=at):
                row = pl.multiple_of((e - low) * 2 * FX, 2 * FX)
                out[pl.ds(row, FX)] = turn_ref[0, e, pl.ds(at, FX), :]
                out[pl.ds(row + FX, FX)] = turn_ref[1, e, pl.ds(at, FX), :]
                return carry

            lax.fori_loop(low, high, copy, 0, unroll=2)


def down_body(own_ref, d_ref, *refs):
    outs, (turn_ref,) = refs[:NX], refs[NX:]
    own = own_ref[0]

    def turn(e, carry):
        turn_ref[e] = flip(d_ref[e])
        return carry

    lax.fori_loop(0, NE, turn, 0, unroll=5)
    for s in range(NX):
        at = pl.multiple_of((own + s) % NX * FX, FX)

        def copy(e, carry, out=outs[s], at=at):
            row = pl.multiple_of(e * FX, FX)
            out[pl.ds(row, FX)] = turn_ref[e, pl.ds(at, FX), :]
            return carry

        lax.fori_loop(0, NE, copy, 0, unroll=3)


def turn_gate_up(own, gate, up):
    sizes = [NE, NE, HEAD, NE, NE - HEAD]
    return pl.pallas_call(
        gate_up_body,
        in_specs=[SMEM, VMEM, VMEM],
        out_specs=[VMEM] * 5,
        out_shape=[jax.ShapeDtypeStruct((n * 2 * FX, GL), BF) for n in sizes],
        scratch_shapes=[pltpu.VMEM((2, NE, FT, GL), BF)],
        compiler_params=pltpu.CompilerParams(vmem_limit_bytes=20 << 20),
        name="turn_gate_up",
    )(own, gate, up)


def turn_down(own, down):
    return pl.pallas_call(
        down_body,
        in_specs=[SMEM, VMEM],
        out_specs=[VMEM] * NX,
        out_shape=[jax.ShapeDtypeStruct((NE * FX, GL), BF)] * NX,
        scratch_shapes=[pltpu.VMEM((NE, FT, GL), BF)],
        compiler_params=pltpu.CompilerParams(vmem_limit_bytes=14 << 20),
        name="turn_down",
    )(own, down)


META = 96
HIGH, LOW, SQ = META + 8, META + 16, META + 24
PR = 4 * ZR
PB = PR + 16


def project_body(z_ref, *refs):
    x_refs, w_refs = refs[:NZ], refs[NZ : NZ + 5]
    p_ref, id_ref, y_ref = refs[NZ + 5 :]
    meta = jnp.concatenate([x[:, 128:256] for x in x_refs], axis=0)
    col = iota((128, TOP * 128), 1)
    pick = (iota((128, TOP * 128), 0) - META == col // 128).astype(F32).astype(BF)
    spread = jnp.dot(meta, pick, preferred_element_type=F32)
    half = (iota((1, TOP * 128), 1) % 128 // 64).astype(F32)
    id_ref[...] = (spread - half).astype(BF)
    xs = []
    for s in range(NX):
        lane = pl.multiple_of((z_ref[NZ] + NX - s) % NX * GL, GL)
        xs.append(jnp.concatenate([x[:, pl.ds(lane, GL)] for x in x_refs], axis=0))
    for start in range(0, NE * 2 * FX, 256):
        size = min(256, NE * 2 * FX - start)
        total = None
        for s in range(NX):
            w_ref, row = w_refs[s], start
            if s == 2 and start >= HEAD * 2 * FX:
                w_ref, row = w_refs[4], start - HEAD * 2 * FX
            part = lax.dot_general(
                xs[s],
                w_ref[row : row + size, :],
                (((1,), (1,)), ((), ())),
                preferred_element_type=F32,
            )
            total = part if total is None else total + part
        y_ref[:, start : start + size] = total.astype(BF)
    low_half = iota((16, 128), 1) < 64

    def body(s, carry):
        r = pl.multiple_of(s * 16, 16)
        z = z_ref[s // 8]
        rr = pl.multiple_of((s % 8) * 16, 16)
        ids = [id_ref[pl.ds(r, 16), j * 128 : (j + 1) * 128] for j in range(TOP)]
        kept = [jnp.zeros((16, 128), BF) for _ in range(TOP)]
        for tile in range(NE // 2):
            y = y_ref[pl.ds(r, 16), tile * 128 : (tile + 1) * 128]
            for j in range(TOP):
                kept[j] = jnp.where(ids[j] == jnp.asarray(2.0 * tile, BF), y, kept[j])
        for q in range(TOP // 2):
            a = kept[2 * q].astype(F32)
            b = kept[2 * q + 1].astype(F32)
            a = a + pltpu.roll(a, 64, 1)
            b = b + pltpu.roll(b, 64, 1)
            p_ref[z, pl.ds(q * ZR + rr, 16), :] = jnp.where(low_half, a, b).astype(BF)
        return carry

    lax.fori_loop(0, ROWS // 16, body, 0)
    for n in range(NZ):
        turned = jnp.transpose(x_refs[n][:, 128:256].astype(F32))
        p_ref[z_ref[n], PR:PB, :] = turned[112:128].astype(BF)


def project(blocks, rows, weights):
    return pl.pallas_call(
        project_body,
        in_specs=[SMEM] + [VMEM] * (NZ + 5),
        out_shape=jax.ShapeDtypeStruct((NZ, PB, 128), BF),
        scratch_shapes=[
            pltpu.VMEM((ROWS, TOP * 128), BF),
            pltpu.VMEM((ROWS, NE * 2 * FX), BF),
        ],
        compiler_params=pltpu.CompilerParams(vmem_limit_bytes=32 << 20),
        name="project",
    )(blocks, *rows, *weights)


def activate_body(p_ref, m_ref, o_ref):
    row = iota((128, 5 * 128), 0)
    col = iota((128, 5 * 128), 1)
    j = 2 * (col // 128) + (col % 128) // 64
    single = jnp.where(row == HIGH + j, 64.0, jnp.where(row == LOW + j, 1.0, 0.0))
    every = jnp.where(
        (row >= HIGH) & (row < LOW), 64.0, jnp.where((row >= LOW) & (row < SQ), 1.0, 0.0)
    )
    pick = jnp.where(col < 512, single, every).astype(BF)
    weights = jnp.dot(m_ref[...], pick, preferred_element_type=F32)
    scale = ROUTE_SCALE / weights[:, 512:640]
    squares = jnp.zeros((16, 128), F32)
    for z in range(NZ):
        squares = squares + p_ref[z, PR:PB, :].astype(F32)
    total = squares[8:9] + squares[9:10]
    inv = lax.rsqrt(total * (1.0 / DIM) + NORM_EPSILON)
    inv = jnp.transpose(jnp.broadcast_to(inv, (128, 128)))
    acts = []
    for q in range(TOP // 2):
        v = jnp.zeros((ZR, 128), F32)
        for z in range(NZ):
            v = v + p_ref[z, q * ZR : (q + 1) * ZR, :].astype(F32)
        v = v * inv
        u = pltpu.roll(v, 128 - FX, 1)
        gate = weights[:, q * 128 : (q + 1) * 128] * scale
        acts.append(v / (1.0 + jnp.exp(-v)) * u * gate)
    first = iota((ZR, 128), 1) % 64 < FX
    for q in range(2):
        packed = jnp.where(first, acts[2 * q], pltpu.roll(acts[2 * q + 1], FX, 1)).astype(BF)
        for z in range(NZ):
            o_ref[z, q * ZR : (q + 1) * ZR, :] = packed


def activate(parts, meta):
    return pl.pallas_call(
        activate_body,
        out_shape=jax.ShapeDtypeStruct((NZ, 2 * ZR, 128), BF),
        compiler_params=pltpu.CompilerParams(vmem_limit_bytes=12 << 20),
        name="activate",
    )(parts, meta)


def combine_body(z_ref, a_ref, *refs):
    x_refs, d_refs = refs[:NZ], refs[NZ : NZ + NX]
    near_ref, far_ref, id_ref, wide_ref, d_ref = refs[NZ + NX :]
    for s in range(NX):
        d_ref[(z_ref[NZ] + NX - s) % NX] = d_refs[s][...]
    meta = jnp.concatenate([x[:, 128:256] for x in x_refs], axis=0)
    row = iota((128, TOP * 128), 0) - META
    col = iota((128, TOP * 128), 1)
    q = col // 512
    k = col // 128 % 4
    block = col % 128 // FX
    origin = (block - k + 4) % 4
    j = 4 * q + jnp.where(origin == 1, 2, jnp.where(origin == 2, 1, origin))
    spread = jnp.dot(meta, (row == j).astype(F32).astype(BF), preferred_element_type=F32)
    id_ref[...] = (spread - (iota((1, TOP * 128), 1) % 128 // FX).astype(F32)).astype(BF)

    def body(s, carry):
        r = pl.multiple_of(s * 16, 16)
        z = z_ref[s // 8]
        rr = pl.multiple_of((s % 8) * 16, 16)
        ids = [id_ref[pl.ds(r, 16), n * 128 : (n + 1) * 128] for n in range(TOP)]
        turned = []
        for n in range(2):
            a = a_ref[z, pl.ds(n * ZR + rr, 16), :].astype(F32)
            for shift in range(4):
                moved = a if shift == 0 else pltpu.roll(a, shift * FX, 1)
                turned.append(moved.astype(BF))
        for g in range(8):
            kept = jnp.zeros((16, 128), BF)
            for n in range(TOP):
                kept = jnp.where(ids[n] == jnp.asarray(4.0 * g, BF), turned[n], kept)
            wide_ref[pl.ds(r, 16), g * 128 : (g + 1) * 128] = kept
        return carry

    lax.fori_loop(0, ROWS // 16, body, 0)
    for x in range(NX):
        out = lax.dot_general(
            wide_ref[:, : NE * FX],
            d_ref[x],
            (((1,), (0,)), ((), ())),
            preferred_element_type=F32,
        )
        out = out[:, :SLICE].astype(BF)
        near_ref[:, x * SLICE : (x + 1) * SLICE] = out[: ROWS // 2]
        far_ref[:, x * SLICE : (x + 1) * SLICE] = out[ROWS // 2 :]


def combine(blocks, acts, rows, down):
    return pl.pallas_call(
        combine_body,
        in_specs=[SMEM] + [VMEM] * (NZ + 1 + NX),
        out_specs=[VMEM] * 2,
        out_shape=[jax.ShapeDtypeStruct((ROWS // 2, WIDE), BF)] * 2,
        scratch_shapes=[
            pltpu.VMEM((ROWS, TOP * 128), BF),
            pltpu.VMEM((ROWS, 1024), BF),
            pltpu.VMEM((NX, NE * FX, GL), BF),
        ],
        compiler_params=pltpu.CompilerParams(vmem_limit_bytes=28 << 20),
        name="combine",
    )(blocks, acts, *rows, *down)


def pack_body(h_ref, n_ref, e_ref, r_ref, l_ref, o_ref):
    widened = h_ref[...].astype(F32)
    scaled = (widened * n_ref[...].astype(F32)).astype(BF)
    squares = jnp.sum(widened * widened, axis=1, keepdims=True)
    high = squares.astype(BF).astype(F32)
    place = iota((RB, NE), 1)
    entries = [
        jnp.sum(
            jnp.where(l_ref[...] == e_ref[:, j : j + 1], place, 0), axis=1, keepdims=True
        ).astype(F32)
        for j in range(TOP)
    ]
    weight = r_ref[...]
    meta = entries + [
        (weight >> 6).astype(F32),
        (weight & 63).astype(F32),
        high,
        squares - high,
        jnp.zeros((RB, GL - SLICE - 26), F32),
    ]
    o_ref[...] = jnp.zeros((RB, NX * GL), BF)
    for k in range(NX):
        o_ref[:, k * GL : k * GL + SLICE] = scaled[:, k * SLICE : (k + 1) * SLICE]
    o_ref[:, SLICE:GL] = jnp.concatenate(meta, axis=1).astype(BF)


def pack_rows(hidden_in, norm_gain, expert_ids, route_weight, updated_list):
    return pl.pallas_call(
        pack_body,
        out_shape=jax.ShapeDtypeStruct((RB, NX * GL), BF),
        compiler_params=pltpu.CompilerParams(vmem_limit_bytes=4 << 20),
        name="pack_rows",
    )(hidden_in, norm_gain[None, :], expert_ids, route_weight, updated_list[None, :])


def gather_rows(packed):
    came = [shift_x(packed, s) for s in range(1, NX)]
    ring = swap_zt(jnp.concatenate([packed] + came, axis=0))
    mine = [ring] + [shift_y(ring, s) for s in range(1, NY)]
    return mine + [other_core(block) for block in mine]


def block_places():
    t = lax.axis_index("tensor")
    y, c = t // 2, t % 2
    s = jnp.arange(NY, dtype=jnp.int32)
    turn = (y - s) % NY * 2
    blocks = jnp.concatenate([turn + c, turn + 1 - c]).astype(jnp.int32)
    zs = jnp.arange(NZ, dtype=jnp.int32)
    places = (y - zs // 2) % NY + NY * (zs % 2 != c).astype(jnp.int32)
    return blocks, places.astype(jnp.int32)


def move_gate_up(pieces):
    ahead = shift_x(pieces[2], 1)
    behind = shift_x(pieces[4], NX - 1)
    came = [pieces[0], shift_x(pieces[1], 1), shift_x(pieces[3], NX - 1)]
    ahead = shift_x(ahead, 1)
    behind = shift_x(behind, NX - 1)
    return [came[0], came[1], ahead, came[2], behind]


def move_down(pieces):
    return [pieces[0]] + [shift_x(pieces[s], s) for s in range(1, NX)]


def place_body(own_ref, *refs):
    pieces, (out_ref, sems) = refs[:NX], refs[NX:]
    copies = [
        pltpu.make_async_copy(
            pieces[s], out_ref.at[:, (own_ref[0] + NX - s) % NX], sems.at[s]
        )
        for s in range(NX)
    ]
    for copy in copies:
        copy.start()
    for copy in copies:
        copy.wait()


def move_gate(chosen, own):
    came = lax.all_to_all(
        chosen.reshape(NZ, NX, SLICE, FT),
        "expert",
        split_axis=0,
        concat_axis=0,
        tiled=True,
        axis_index_groups=Z_GROUPS,
    )
    x = own[0]
    pieces = [
        lax.dynamic_index_in_dim(came, (x + s) % NX, 1, keepdims=False) for s in range(NX)
    ]
    pieces = [pieces[0]] + [shift_x(pieces[s], s) for s in range(1, NX)]
    anywhere = pl.BlockSpec(memory_space=pl.ANY)
    return pl.pallas_call(
        place_body,
        in_specs=[SMEM] + [anywhere] * NX,
        out_specs=anywhere,
        out_shape=jax.ShapeDtypeStruct((NZ, NX, SLICE, FT), BF),
        scratch_shapes=[pltpu.SemaphoreType.DMA((NX,))],
        compiler_params=pltpu.CompilerParams(vmem_limit_bytes=1 << 20),
        name="place_gate",
    )(own, *pieces).reshape(1, DIM, FT)


def add(values):
    total = values[0].astype(F32)
    for value in values[1:]:
        total = total + value.astype(F32)
    return total.astype(BF)


def gather_out(near, far):
    size = near.shape[0] // NY
    blocks = [
        add([near[s * size : (s + 1) * size], far[s * size : (s + 1) * size]]) for s in range(NY)
    ]
    came = [blocks[0]] + [shift_y(blocks[s], NY - s) for s in range(1, NY)]
    pieces = [add([b[s * RB : (s + 1) * RB] for b in came]) for s in range(NX)]
    came = [pieces[0]] + [shift_x(pieces[s], NX - s) for s in range(1, NX)]
    return swap_zt(add(came))


def device_body(
    query_latent,
    kv_cache,
    cache_len,
    value_up,
    hidden_in,
    norm_gain,
    expert_ids,
    route_weight,
    placement_plan,
    updated_list,
    learner_gate,
    learner_up,
    learner_down,
):
    own = (lax.axis_index("expert") % NX).astype(jnp.int32)[None]
    held = move_gate_up(turn_gate_up(own, learner_gate, learner_up))
    rows = gather_rows(pack_rows(hidden_in, norm_gain, expert_ids, route_weight, updated_list))
    blocks, places = block_places()
    blocks = jnp.concatenate([blocks, own])

    entry_range = jnp.arange(NE, dtype=jnp.int32)
    learner_entry = jnp.sum(
        entry_range[None, :] * (updated_list[None, :] == placement_plan[:, None]).astype(jnp.int32),
        axis=1,
    )
    slot_gate = move_gate(jnp.take(learner_gate, learner_entry, axis=0, mode="clip"), own)

    held_down = move_down(turn_down(own, learner_down))
    parts = exchange(project(blocks, rows, held), Z_GROUPS)
    z = lax.axis_index("expert") // NX
    metas = jnp.stack([block[:, 128:256] for block in rows])
    meta = lax.dynamic_index_in_dim(metas, places[z], 0, keepdims=False)
    acts = exchange(activate(parts, meta), Z_GROUPS)
    near, far = combine(blocks, acts, rows, held_down)
    far = other_core(far)
    moe_out = gather_out(near, far)

    latent = attend(query_latent, kv_cache, cache_len)
    head_rows = lax.all_to_all(latent, "tensor", split_axis=1, concat_axis=0, tiled=True)
    projected = jnp.einsum("rhc,hcv->rhv", head_rows, value_up, preferred_element_type=F32)
    attn_values = projected.astype(BF).reshape(
        head_rows.shape[0], projected.shape[1] * projected.shape[2]
    )
    return (attn_values, moe_out, slot_gate)


def solution(mesh):
    in_specs = (
        P(("expert", "tensor"), None, None),
        P(("expert", "tensor"), None, None),
        P(("expert", "tensor")),
        P("tensor", None, None),
        P("expert", "tensor"),
        P("tensor"),
        P("expert", None),
        P("expert", None),
        P(),
        P(),
        P(None, "expert", "tensor"),
        P(None, "expert", "tensor"),
        P(None, "expert", "tensor"),
    )
    out_specs = (P("expert", "tensor"), P("expert", "tensor"), P("expert", None, "tensor"))
    return jax.shard_map(
        device_body, mesh=mesh, in_specs=in_specs, out_specs=out_specs, check_vma=False
    )
```

```python
import jax
import jax.numpy as jnp
from jax import lax
from jax.experimental import pallas as pl
from jax.experimental.pallas import tpu as pltpu
from jax.sharding import PartitionSpec as P


KVL = 512
SCORE_SCALE = 192.0 ** (-0.5)
ROUTE_SCALE = 2.5
NORM_EPSILON = 1e-06

NZ, NX, NT, NY = 8, 4, 8, 4
RB = 32
ZR = NX * RB
ROWS = NZ * ZR
SLICE = 224
WIDE = NX * SLICE
GL = 256
FT = 128
FX = FT // NX
NE = 30
TOP = 8
DIM = 7168

Z_GROUPS = [[z * NX + x for z in range(NZ)] for x in range(NX)]
SWAP = [
    ((z * NX + x) * NT + t, (t * NX + x) * NT + z)
    for z in range(NZ)
    for x in range(NX)
    for t in range(NT)
]
BF = jnp.bfloat16
F32 = jnp.float32


def swap_zt(value):
    return lax.ppermute(value, ("expert", "tensor"), SWAP)


def exchange(value, groups):
    return lax.all_to_all(
        value, "expert", split_axis=0, concat_axis=0, tiled=True, axis_index_groups=groups
    )


def shift_x(value, step):
    pairs = [(z * NX + x, z * NX + (x + step) % NX) for z in range(NZ) for x in range(NX)]
    return lax.ppermute(value, "expert", pairs)


def shift_y(value, step):
    pairs = [(y * 2 + c, (y + step) % NY * 2 + c) for y in range(NY) for c in range(2)]
    return lax.ppermute(value, "tensor", pairs)


def other_core(value):
    return lax.ppermute(value, "tensor", [(t, t ^ 1) for t in range(NT)])


def attend(query_latent, kv_cache, cache_len):
    scores = (
        jnp.einsum("rhc,rpc->rhp", query_latent, kv_cache, preferred_element_type=F32)
        * SCORE_SCALE
    )
    allowed = (jnp.arange(kv_cache.shape[1], dtype=jnp.int32)[None, :] < cache_len[:, None])[
        :, None, :
    ]
    scores = jnp.where(allowed, scores, -1e30)
    highest = jnp.max(scores, axis=2, keepdims=True)
    lifted = jnp.where(allowed, jnp.exp(scores - highest), 0.0)
    totals = jnp.sum(lifted, axis=2, keepdims=True)
    mixed = jnp.einsum(
        "rhp,rpc->rhc",
        lifted.astype(BF),
        kv_cache[:, :, :KVL],
        preferred_element_type=F32,
    )
    return (mixed / totals).astype(BF)


def iota(shape, axis):
    return lax.broadcasted_iota(jnp.int32, shape, axis)


def flip(block):
    turned = jnp.transpose(block.astype(F32))
    return jnp.concatenate([turned, jnp.zeros((FT, GL - SLICE), F32)], axis=1).astype(BF)


SMEM = pl.BlockSpec(memory_space=pltpu.SMEM)
VMEM = pl.BlockSpec(memory_space=pltpu.VMEM)
HEAD = 16


def gate_up_body(own_ref, g_ref, u_ref, *refs):
    outs, (turn_ref,) = refs[:5], refs[5:]
    own = own_ref[0]

    def turn(e, carry):
        turn_ref[0, e] = flip(g_ref[e])
        turn_ref[1, e] = flip(u_ref[e])
        return carry

    lax.fori_loop(0, NE, turn, 0, unroll=5)
    for s in range(NX):
        at = pl.multiple_of((own + s) % NX * FX, FX)
        spans = [(outs[s], 0, NE)]
        if s == 2:
            spans = [(outs[2], 0, HEAD), (outs[4], HEAD, NE)]
        for out, low, high in spans:

            def copy(e, carry, out=out, low=low, at=at):
                row = pl.multiple_of((e - low) * 2 * FX, 2 * FX)
                out[pl.ds(row, FX)] = turn_ref[0, e, pl.ds(at, FX), :]
                out[pl.ds(row + FX, FX)] = turn_ref[1, e, pl.ds(at, FX), :]
                return carry

            lax.fori_loop(low, high, copy, 0, unroll=2)


def down_body(own_ref, d_ref, *refs):
    outs, (turn_ref,) = refs[:NX], refs[NX:]
    own = own_ref[0]

    def turn(e, carry):
        turn_ref[e] = flip(d_ref[e])
        return carry

    lax.fori_loop(0, NE, turn, 0, unroll=5)
    for s in range(NX):
        at = pl.multiple_of((own + s) % NX * FX, FX)

        def copy(e, carry, out=outs[s], at=at):
            row = pl.multiple_of(e * FX, FX)
            out[pl.ds(row, FX)] = turn_ref[e, pl.ds(at, FX), :]
            return carry

        lax.fori_loop(0, NE, copy, 0, unroll=3)


def turn_gate_up(own, gate, up):
    sizes = [NE, NE, HEAD, NE, NE - HEAD]
    return pl.pallas_call(
        gate_up_body,
        in_specs=[SMEM, VMEM, VMEM],
        out_specs=[VMEM] * 5,
        out_shape=[jax.ShapeDtypeStruct((n * 2 * FX, GL), BF) for n in sizes],
        scratch_shapes=[pltpu.VMEM((2, NE, FT, GL), BF)],
        compiler_params=pltpu.CompilerParams(vmem_limit_bytes=20 << 20),
        name="turn_gate_up",
    )(own, gate, up)


def turn_down(own, down):
    return pl.pallas_call(
        down_body,
        in_specs=[SMEM, VMEM],
        out_specs=[VMEM] * NX,
        out_shape=[jax.ShapeDtypeStruct((NE * FX, GL), BF)] * NX,
        scratch_shapes=[pltpu.VMEM((NE, FT, GL), BF)],
        compiler_params=pltpu.CompilerParams(vmem_limit_bytes=14 << 20),
        name="turn_down",
    )(own, down)


META = 96
HIGH, LOW, SQ = META + 8, META + 16, META + 24
PR = 4 * ZR
PB = PR + 16


def project_body(z_ref, *refs):
    x_refs, w_refs = refs[:NZ], refs[NZ : NZ + 5]
    p_ref, id_ref, y_ref = refs[NZ + 5 :]
    meta = jnp.concatenate([x[:, 128:256] for x in x_refs], axis=0)
    col = iota((128, TOP * 128), 1)
    pick = (iota((128, TOP * 128), 0) - META == col // 128).astype(F32).astype(BF)
    spread = jnp.dot(meta, pick, preferred_element_type=F32)
    half = (iota((1, TOP * 128), 1) % 128 // 64).astype(F32)
    tags = (spread - half).astype(BF)
    for j in range(TOP):
        id_ref[j] = tags[:, j * 128 : (j + 1) * 128]
    xs = []
    for s in range(NX):
        lane = pl.multiple_of((z_ref[NZ] + NX - s) % NX * GL, GL)
        xs.append(jnp.concatenate([x[:, pl.ds(lane, GL)] for x in x_refs], axis=0))
    for start in range(0, NE * 2 * FX, 256):
        size = min(256, NE * 2 * FX - start)
        total = None
        for s in range(NX):
            w_ref, row = w_refs[s], start
            if s == 2 and start >= HEAD * 2 * FX:
                w_ref, row = w_refs[4], start - HEAD * 2 * FX
            part = lax.dot_general(
                xs[s],
                w_ref[row : row + size, :],
                (((1,), (1,)), ((), ())),
                preferred_element_type=F32,
            )
            total = part if total is None else total + part
        total = total.astype(BF)
        for n in range(size // 128):
            y_ref[start // 128 + n] = total[:, n * 128 : (n + 1) * 128]
    low_half = iota((16, 128), 1) < 64

    def body(s, carry):
        r = pl.multiple_of(s * 16, 16)
        z = z_ref[s // 8]
        rr = pl.multiple_of((s % 8) * 16, 16)
        ids = [id_ref[j, pl.ds(r, 16), :] for j in range(TOP)]
        kept = [jnp.zeros((16, 128), BF) for _ in range(TOP)]
        for tile in range(NE // 2):
            y = y_ref[tile, pl.ds(r, 16), :]
            for j in range(TOP):
                kept[j] = jnp.where(ids[j] == jnp.asarray(2.0 * tile, BF), y, kept[j])
        for q in range(TOP // 2):
            a = kept[2 * q].astype(F32)
            b = kept[2 * q + 1].astype(F32)
            a = a + pltpu.roll(a, 64, 1)
            b = b + pltpu.roll(b, 64, 1)
            p_ref[z, pl.ds(q * ZR + rr, 16), :] = jnp.where(low_half, a, b).astype(BF)
        return carry

    lax.fori_loop(0, ROWS // 16, body, 0, unroll=4)
    for n in range(NZ):
        turned = jnp.transpose(x_refs[n][:, 128:256].astype(F32))
        p_ref[z_ref[n], PR:PB, :] = turned[112:128].astype(BF)


def project(blocks, rows, weights):
    return pl.pallas_call(
        project_body,
        in_specs=[SMEM] + [VMEM] * (NZ + 5),
        out_shape=jax.ShapeDtypeStruct((NZ, PB, 128), BF),
        scratch_shapes=[
            pltpu.VMEM((TOP, ROWS, 128), BF),
            pltpu.VMEM((NE // 2, ROWS, 128), BF),
        ],
        compiler_params=pltpu.CompilerParams(vmem_limit_bytes=32 << 20),
        name="project",
    )(blocks, *rows, *weights)


def activate_body(p_ref, m_ref, o_ref):
    row = iota((128, 5 * 128), 0)
    col = iota((128, 5 * 128), 1)
    j = 2 * (col // 128) + (col % 128) // 64
    single = jnp.where(row == HIGH + j, 64.0, jnp.where(row == LOW + j, 1.0, 0.0))
    every = jnp.where(
        (row >= HIGH) & (row < LOW), 64.0, jnp.where((row >= LOW) & (row < SQ), 1.0, 0.0)
    )
    pick = jnp.where(col < 512, single, every).astype(BF)
    weights = jnp.dot(m_ref[...], pick, preferred_element_type=F32)
    scale = ROUTE_SCALE / weights[:, 512:640]
    squares = jnp.zeros((16, 128), F32)
    for z in range(NZ):
        squares = squares + p_ref[z, PR:PB, :].astype(F32)
    total = squares[8:9] + squares[9:10]
    inv = lax.rsqrt(total * (1.0 / DIM) + NORM_EPSILON)
    inv = jnp.transpose(jnp.broadcast_to(inv, (128, 128)))
    acts = []
    for q in range(TOP // 2):
        v = jnp.zeros((ZR, 128), F32)
        for z in range(NZ):
            v = v + p_ref[z, q * ZR : (q + 1) * ZR, :].astype(F32)
        v = v * inv
        u = pltpu.roll(v, 128 - FX, 1)
        gate = weights[:, q * 128 : (q + 1) * 128] * scale
        acts.append(v / (1.0 + jnp.exp(-v)) * u * gate)
    first = iota((ZR, 128), 1) % 64 < FX
    for q in range(2):
        packed = jnp.where(first, acts[2 * q], pltpu.roll(acts[2 * q + 1], FX, 1)).astype(BF)
        for z in range(NZ):
            o_ref[z, q * ZR : (q + 1) * ZR, :] = packed


def activate(parts, meta):
    return pl.pallas_call(
        activate_body,
        out_shape=jax.ShapeDtypeStruct((NZ, 2 * ZR, 128), BF),
        compiler_params=pltpu.CompilerParams(vmem_limit_bytes=12 << 20),
        name="activate",
    )(parts, meta)


def combine_body(z_ref, a_ref, m_ref, *refs):
    d_refs = refs[:NX]
    near_ref, far_ref, id_ref, wide_ref, d_ref = refs[NX:]
    for s in range(NX):
        d_ref[(z_ref[NZ] + NX - s) % NX] = d_refs[s][...]
    row = iota((128, TOP * 128), 0) - META
    col = iota((128, TOP * 128), 1)
    q = col // 512
    k = col // 128 % 4
    block = col % 128 // FX
    origin = (block - k + 4) % 4
    j = 4 * q + jnp.where(origin == 1, 2, jnp.where(origin == 2, 1, origin))
    spread = jnp.dot(m_ref[...], (row == j).astype(F32).astype(BF), preferred_element_type=F32)
    tags = (spread - (iota((1, TOP * 128), 1) % 128 // FX).astype(F32)).astype(BF)
    for n in range(TOP):
        id_ref[n] = tags[:, n * 128 : (n + 1) * 128]

    def body(s, carry):
        r = pl.multiple_of(s * 16, 16)
        z = z_ref[s // 8]
        rr = pl.multiple_of((s % 8) * 16, 16)
        ids = [id_ref[n, pl.ds(r, 16), :] for n in range(TOP)]
        turned = []
        for n in range(2):
            a = a_ref[z, pl.ds(n * ZR + rr, 16), :].astype(F32)
            for shift in range(4):
                moved = a if shift == 0 else pltpu.roll(a, shift * FX, 1)
                turned.append(moved.astype(BF))
        for g in range(8):
            kept = jnp.zeros((16, 128), BF)
            for n in range(TOP):
                kept = jnp.where(ids[n] == jnp.asarray(4.0 * g, BF), turned[n], kept)
            wide_ref[g, pl.ds(r, 16), :] = kept
        return carry

    lax.fori_loop(0, ROWS // 16, body, 0, unroll=4)
    for x in range(NX):
        out = None
        for g in range(0, 8, 2):
            width = min(256, NE * FX - g * 128)
            wide = jnp.concatenate([wide_ref[g], wide_ref[g + 1]], axis=1)
            part = jnp.dot(
                wide[:, :width],
                d_ref[x, g * 128 : g * 128 + width],
                preferred_element_type=F32,
            )
            out = part if out is None else out + part
        out = out[:, :SLICE].astype(BF)
        near_ref[:, x * SLICE : (x + 1) * SLICE] = out[: ROWS // 2]
        far_ref[:, x * SLICE : (x + 1) * SLICE] = out[ROWS // 2 :]


def combine(blocks, acts, metas, down):
    return pl.pallas_call(
        combine_body,
        in_specs=[SMEM] + [VMEM] * (2 + NX),
        out_specs=[VMEM] * 2,
        out_shape=[jax.ShapeDtypeStruct((ROWS // 2, WIDE), BF)] * 2,
        scratch_shapes=[
            pltpu.VMEM((TOP, ROWS, 128), BF),
            pltpu.VMEM((8, ROWS, 128), BF),
            pltpu.VMEM((NX, NE * FX, GL), BF),
        ],
        compiler_params=pltpu.CompilerParams(vmem_limit_bytes=28 << 20),
        name="combine",
    )(blocks, acts, metas, *down)


def pack_body(h_ref, n_ref, e_ref, r_ref, l_ref, o_ref):
    widened = h_ref[...].astype(F32)
    scaled = (widened * n_ref[...].astype(F32)).astype(BF)
    squares = jnp.sum(widened * widened, axis=1, keepdims=True)
    high = squares.astype(BF).astype(F32)
    place = iota((RB, NE), 1)
    entries = [
        jnp.sum(
            jnp.where(l_ref[...] == e_ref[:, j : j + 1], place, 0), axis=1, keepdims=True
        ).astype(F32)
        for j in range(TOP)
    ]
    weight = r_ref[...]
    meta = entries + [
        (weight >> 6).astype(F32),
        (weight & 63).astype(F32),
        high,
        squares - high,
        jnp.zeros((RB, GL - SLICE - 26), F32),
    ]
    o_ref[...] = jnp.zeros((RB, NX * GL), BF)
    for k in range(NX):
        o_ref[:, k * GL : k * GL + SLICE] = scaled[:, k * SLICE : (k + 1) * SLICE]
    o_ref[:, SLICE:GL] = jnp.concatenate(meta, axis=1).astype(BF)


def pack_rows(hidden_in, norm_gain, expert_ids, route_weight, updated_list):
    return pl.pallas_call(
        pack_body,
        out_shape=jax.ShapeDtypeStruct((RB, NX * GL), BF),
        compiler_params=pltpu.CompilerParams(vmem_limit_bytes=4 << 20),
        name="pack_rows",
    )(hidden_in, norm_gain[None, :], expert_ids, route_weight, updated_list[None, :])


def gather_rows(packed):
    came = [shift_x(packed, s) for s in range(1, NX)]
    ring = swap_zt(jnp.concatenate([packed] + came, axis=0))
    mine = [ring] + [shift_y(ring, s) for s in range(1, NY)]
    return mine + [other_core(block) for block in mine]


def block_places():
    t = lax.axis_index("tensor")
    y, c = t // 2, t % 2
    s = jnp.arange(NY, dtype=jnp.int32)
    turn = (y - s) % NY * 2
    blocks = jnp.concatenate([turn + c, turn + 1 - c]).astype(jnp.int32)
    zs = jnp.arange(NZ, dtype=jnp.int32)
    places = (y - zs // 2) % NY + NY * (zs % 2 != c).astype(jnp.int32)
    return blocks, places.astype(jnp.int32)


def move_gate_up(pieces):
    ahead = shift_x(pieces[2], 1)
    behind = shift_x(pieces[4], NX - 1)
    came = [pieces[0], shift_x(pieces[1], 1), shift_x(pieces[3], NX - 1)]
    ahead = shift_x(ahead, 1)
    behind = shift_x(behind, NX - 1)
    return [came[0], came[1], ahead, came[2], behind]


def move_down(pieces):
    return [pieces[0]] + [shift_x(pieces[s], s) for s in range(1, NX)]


def place_body(own_ref, *refs):
    pieces, (out_ref,) = refs[:NX], refs[NX:]
    for s in range(NX):
        out_ref[:, (own_ref[0] + NX - s) % NX] = pieces[s][...]


def move_gate(chosen, own):
    came = lax.all_to_all(
        chosen.reshape(NZ, NX, SLICE, FT),
        "expert",
        split_axis=0,
        concat_axis=0,
        tiled=True,
        axis_index_groups=Z_GROUPS,
    )
    x = own[0]
    pieces = [
        lax.dynamic_index_in_dim(came, (x + s) % NX, 1, keepdims=False) for s in range(NX)
    ]
    pieces = [pieces[0]] + [shift_x(pieces[s], s) for s in range(1, NX)]
    return pl.pallas_call(
        place_body,
        in_specs=[SMEM] + [VMEM] * NX,
        out_specs=VMEM,
        out_shape=jax.ShapeDtypeStruct((NZ, NX, SLICE, FT), BF),
        compiler_params=pltpu.CompilerParams(vmem_limit_bytes=8 << 20),
        name="place_gate",
    )(own, *pieces).reshape(1, DIM, FT)


def add(values):
    total = values[0].astype(F32)
    for value in values[1:]:
        total = total + value.astype(F32)
    return total.astype(BF)


def gather_out(near, far):
    size = near.shape[0] // NY
    blocks = [
        add([near[s * size : (s + 1) * size], far[s * size : (s + 1) * size]]) for s in range(NY)
    ]
    came = [blocks[0]] + [shift_y(blocks[s], NY - s) for s in range(1, NY)]
    pieces = [add([b[s * RB : (s + 1) * RB] for b in came]) for s in range(NX)]
    came = [pieces[0]] + [shift_x(pieces[s], NX - s) for s in range(1, NX)]
    return swap_zt(add(came))


def device_body(
    query_latent,
    kv_cache,
    cache_len,
    value_up,
    hidden_in,
    norm_gain,
    expert_ids,
    route_weight,
    placement_plan,
    updated_list,
    learner_gate,
    learner_up,
    learner_down,
):
    own = (lax.axis_index("expert") % NX).astype(jnp.int32)[None]
    held = move_gate_up(turn_gate_up(own, learner_gate, learner_up))
    rows = gather_rows(pack_rows(hidden_in, norm_gain, expert_ids, route_weight, updated_list))
    blocks, places = block_places()
    blocks = jnp.concatenate([blocks, own])

    entry_range = jnp.arange(NE, dtype=jnp.int32)
    learner_entry = jnp.sum(
        entry_range[None, :] * (updated_list[None, :] == placement_plan[:, None]).astype(jnp.int32),
        axis=1,
    )
    slot_gate = move_gate(jnp.take(learner_gate, learner_entry, axis=0, mode="clip"), own)

    held_down = move_down(turn_down(own, learner_down))
    parts = exchange(project(blocks, rows, held), Z_GROUPS)
    z = lax.axis_index("expert") // NX
    metas = jnp.stack([block[:, 128:256] for block in rows])
    meta = lax.dynamic_index_in_dim(metas, places[z], 0, keepdims=False)
    acts = exchange(activate(parts, meta), Z_GROUPS)
    near, far = combine(blocks, acts, metas.reshape(ROWS, 128), held_down)
    far = other_core(far)
    moe_out = gather_out(near, far)

    latent = attend(query_latent, kv_cache, cache_len)
    head_rows = lax.all_to_all(latent, "tensor", split_axis=1, concat_axis=0, tiled=True)
    projected = jnp.einsum("rhc,hcv->rhv", head_rows, value_up, preferred_element_type=F32)
    attn_values = projected.astype(BF).reshape(
        head_rows.shape[0], projected.shape[1] * projected.shape[2]
    )
    return (attn_values, moe_out, slot_gate)


def solution(mesh):
    in_specs = (
        P(("expert", "tensor"), None, None),
        P(("expert", "tensor"), None, None),
        P(("expert", "tensor")),
        P("tensor", None, None),
        P("expert", "tensor"),
        P("tensor"),
        P("expert", None),
        P("expert", None),
        P(),
        P(),
        P(None, "expert", "tensor"),
        P(None, "expert", "tensor"),
        P(None, "expert", "tensor"),
    )
    out_specs = (P("expert", "tensor"), P("expert", "tensor"), P("expert", None, "tensor"))
    return jax.shard_map(
        device_body, mesh=mesh, in_specs=in_specs, out_specs=out_specs, check_vma=False
    )
```

```python
import jax
import jax.numpy as jnp
from jax import lax
from jax.experimental import pallas as pl
from jax.experimental.pallas import tpu as pltpu
from jax.sharding import PartitionSpec as P


KVL = 512
SCORE_SCALE = 192.0 ** (-0.5)
ROUTE_SCALE = 2.5
NORM_EPSILON = 1e-06

NZ, NX, NT, NY = 8, 4, 8, 4
RB = 32
ZR = NX * RB
ROWS = NZ * ZR
SLICE = 224
WIDE = NX * SLICE
GL = 256
FT = 128
FX = FT // NX
NE = 30
TOP = 8
DIM = 7168

Z_GROUPS = [[z * NX + x for z in range(NZ)] for x in range(NX)]
SWAP = [
    ((z * NX + x) * NT + t, (t * NX + x) * NT + z)
    for z in range(NZ)
    for x in range(NX)
    for t in range(NT)
]
BF = jnp.bfloat16
F32 = jnp.float32


def swap_zt(value):
    return lax.ppermute(value, ("expert", "tensor"), SWAP)


def exchange(value, groups):
    return lax.all_to_all(
        value, "expert", split_axis=0, concat_axis=0, tiled=True, axis_index_groups=groups
    )


def shift_x(value, step):
    pairs = [(z * NX + x, z * NX + (x + step) % NX) for z in range(NZ) for x in range(NX)]
    return lax.ppermute(value, "expert", pairs)


def shift_y(value, step):
    pairs = [(y * 2 + c, (y + step) % NY * 2 + c) for y in range(NY) for c in range(2)]
    return lax.ppermute(value, "tensor", pairs)


def other_core(value):
    return lax.ppermute(value, "tensor", [(t, t ^ 1) for t in range(NT)])


def attend(query_latent, kv_cache, cache_len):
    scores = (
        jnp.einsum("rhc,rpc->rhp", query_latent, kv_cache, preferred_element_type=F32)
        * SCORE_SCALE
    )
    allowed = (jnp.arange(kv_cache.shape[1], dtype=jnp.int32)[None, :] < cache_len[:, None])[
        :, None, :
    ]
    scores = jnp.where(allowed, scores, -1e30)
    highest = jnp.max(scores, axis=2, keepdims=True)
    lifted = jnp.where(allowed, jnp.exp(scores - highest), 0.0)
    totals = jnp.sum(lifted, axis=2, keepdims=True)
    mixed = jnp.einsum(
        "rhp,rpc->rhc",
        lifted.astype(BF),
        kv_cache[:, :, :KVL],
        preferred_element_type=F32,
    )
    return (mixed / totals).astype(BF)


def iota(shape, axis):
    return lax.broadcasted_iota(jnp.int32, shape, axis)


def flip(block):
    turned = jnp.transpose(block.astype(F32))
    return jnp.concatenate([turned, jnp.zeros((FT, GL - SLICE), F32)], axis=1).astype(BF)


SMEM = pl.BlockSpec(memory_space=pltpu.SMEM)
VMEM = pl.BlockSpec(memory_space=pltpu.VMEM)
HEAD = 16


def gate_up_body(own_ref, g_ref, u_ref, *refs):
    outs, (turn_ref,) = refs[:5], refs[5:]
    own = own_ref[0]

    def turn(e, carry):
        turn_ref[0, e] = flip(g_ref[e])
        turn_ref[1, e] = flip(u_ref[e])
        return carry

    lax.fori_loop(0, NE, turn, 0, unroll=5)
    for s in range(NX):
        at = pl.multiple_of((own + s) % NX * FX, FX)
        spans = [(outs[s], 0, NE)]
        if s == 2:
            spans = [(outs[2], 0, HEAD), (outs[4], HEAD, NE)]
        for out, low, high in spans:

            def copy(e, carry, out=out, low=low, at=at):
                row = pl.multiple_of((e - low) * 2 * FX, 2 * FX)
                out[pl.ds(row, FX)] = turn_ref[0, e, pl.ds(at, FX), :]
                out[pl.ds(row + FX, FX)] = turn_ref[1, e, pl.ds(at, FX), :]
                return carry

            lax.fori_loop(low, high, copy, 0, unroll=2)


def down_body(own_ref, d_ref, *refs):
    outs, (turn_ref,) = refs[:NX], refs[NX:]
    own = own_ref[0]

    def turn(e, carry):
        turn_ref[e] = flip(d_ref[e])
        return carry

    lax.fori_loop(0, NE, turn, 0, unroll=5)
    for s in range(NX):
        at = pl.multiple_of((own + s) % NX * FX, FX)

        def copy(e, carry, out=outs[s], at=at):
            row = pl.multiple_of(e * FX, FX)
            out[pl.ds(row, FX)] = turn_ref[e, pl.ds(at, FX), :]
            return carry

        lax.fori_loop(0, NE, copy, 0, unroll=3)


def turn_gate_up(own, gate, up):
    sizes = [NE, NE, HEAD, NE, NE - HEAD]
    return pl.pallas_call(
        gate_up_body,
        in_specs=[SMEM, VMEM, VMEM],
        out_specs=[VMEM] * 5,
        out_shape=[jax.ShapeDtypeStruct((n * 2 * FX, GL), BF) for n in sizes],
        scratch_shapes=[pltpu.VMEM((2, NE, FT, GL), BF)],
        compiler_params=pltpu.CompilerParams(vmem_limit_bytes=20 << 20),
        name="turn_gate_up",
    )(own, gate, up)


def turn_down(own, down):
    return pl.pallas_call(
        down_body,
        in_specs=[SMEM, VMEM],
        out_specs=[VMEM] * NX,
        out_shape=[jax.ShapeDtypeStruct((NE * FX, GL), BF)] * NX,
        scratch_shapes=[pltpu.VMEM((NE, FT, GL), BF)],
        compiler_params=pltpu.CompilerParams(vmem_limit_bytes=14 << 20),
        name="turn_down",
    )(own, down)


META = 96
HIGH, LOW, SQ = META + 8, META + 16, META + 24
PR = 4 * ZR
PB = PR + 16


def project_body(z_ref, *refs):
    x_refs, w_refs = refs[:NZ], refs[NZ : NZ + 5]
    p_ref, id_ref, y_ref = refs[NZ + 5 :]
    meta = jnp.concatenate([x[:, 128:256] for x in x_refs], axis=0)
    col = iota((128, TOP * 128), 1)
    pick = (iota((128, TOP * 128), 0) - META == col // 128).astype(F32).astype(BF)
    spread = jnp.dot(meta, pick, preferred_element_type=F32)
    half = (iota((1, TOP * 128), 1) % 128 // 64).astype(F32)
    tags = (spread - half).astype(BF)
    for j in range(TOP):
        id_ref[j] = tags[:, j * 128 : (j + 1) * 128]
    xs = []
    for s in range(NX):
        lane = pl.multiple_of((z_ref[NZ] + NX - s) % NX * GL, GL)
        xs.append(jnp.concatenate([x[:, pl.ds(lane, GL)] for x in x_refs], axis=0))
    for start in range(0, NE * 2 * FX, 256):
        size = min(256, NE * 2 * FX - start)
        total = None
        for s in range(NX):
            w_ref, row = w_refs[s], start
            if s == 2 and start >= HEAD * 2 * FX:
                w_ref, row = w_refs[4], start - HEAD * 2 * FX
            part = lax.dot_general(
                xs[s],
                w_ref[row : row + size, :],
                (((1,), (1,)), ((), ())),
                preferred_element_type=F32,
            )
            total = part if total is None else total + part
        total = total.astype(BF)
        for n in range(size // 128):
            y_ref[start // 128 + n] = total[:, n * 128 : (n + 1) * 128]
    low_half = iota((16, 128), 1) < 64

    def body(s, carry):
        r = pl.multiple_of(s * 16, 16)
        z = z_ref[s // 8]
        rr = pl.multiple_of((s % 8) * 16, 16)
        ids = [id_ref[j, pl.ds(r, 16), :] for j in range(TOP)]
        kept = [jnp.zeros((16, 128), BF) for _ in range(TOP)]
        for tile in range(NE // 2):
            y = y_ref[tile, pl.ds(r, 16), :]
            for j in range(TOP):
                kept[j] = jnp.where(ids[j] == jnp.asarray(2.0 * tile, BF), y, kept[j])
        for q in range(TOP // 2):
            a = kept[2 * q].astype(F32)
            b = kept[2 * q + 1].astype(F32)
            a = a + pltpu.roll(a, 64, 1)
            b = b + pltpu.roll(b, 64, 1)
            p_ref[z, pl.ds(q * ZR + rr, 16), :] = jnp.where(low_half, a, b).astype(BF)
        return carry

    lax.fori_loop(0, ROWS // 16, body, 0, unroll=4)
    for n in range(NZ):
        turned = jnp.transpose(x_refs[n][:, 128:256].astype(F32))
        p_ref[z_ref[n], PR:PB, :] = turned[112:128].astype(BF)


def project(blocks, rows, weights):
    return pl.pallas_call(
        project_body,
        in_specs=[SMEM] + [VMEM] * (NZ + 5),
        out_shape=jax.ShapeDtypeStruct((NZ, PB, 128), BF),
        scratch_shapes=[
            pltpu.VMEM((TOP, ROWS, 128), BF),
            pltpu.VMEM((NE // 2, ROWS, 128), BF),
        ],
        compiler_params=pltpu.CompilerParams(vmem_limit_bytes=32 << 20),
        name="project",
    )(blocks, *rows, *weights)


def activate_body(p_ref, m_ref, o_ref):
    row = iota((128, 5 * 128), 0)
    col = iota((128, 5 * 128), 1)
    j = 2 * (col // 128) + (col % 128) // 64
    single = jnp.where(row == HIGH + j, 64.0, jnp.where(row == LOW + j, 1.0, 0.0))
    every = jnp.where(
        (row >= HIGH) & (row < LOW), 64.0, jnp.where((row >= LOW) & (row < SQ), 1.0, 0.0)
    )
    pick = jnp.where(col < 512, single, every).astype(BF)
    weights = jnp.dot(m_ref[...], pick, preferred_element_type=F32)
    scale = ROUTE_SCALE / weights[:, 512:640]
    squares = jnp.zeros((16, 128), F32)
    for z in range(NZ):
        squares = squares + p_ref[z, PR:PB, :].astype(F32)
    total = squares[8:9] + squares[9:10]
    inv = lax.rsqrt(total * (1.0 / DIM) + NORM_EPSILON)
    inv = jnp.transpose(jnp.broadcast_to(inv, (128, 128)))
    acts = []
    for q in range(TOP // 2):
        v = jnp.zeros((ZR, 128), F32)
        for z in range(NZ):
            v = v + p_ref[z, q * ZR : (q + 1) * ZR, :].astype(F32)
        v = v * inv
        u = pltpu.roll(v, 128 - FX, 1)
        gate = weights[:, q * 128 : (q + 1) * 128] * scale
        acts.append(v / (1.0 + jnp.exp(-v)) * u * gate)
    first = iota((ZR, 128), 1) % 64 < FX
    for q in range(2):
        packed = jnp.where(first, acts[2 * q], pltpu.roll(acts[2 * q + 1], FX, 1)).astype(BF)
        for z in range(NZ):
            o_ref[z, q * ZR : (q + 1) * ZR, :] = packed


def activate(parts, meta):
    return pl.pallas_call(
        activate_body,
        out_shape=jax.ShapeDtypeStruct((NZ, 2 * ZR, 128), BF),
        compiler_params=pltpu.CompilerParams(vmem_limit_bytes=12 << 20),
        name="activate",
    )(parts, meta)


def combine_body(z_ref, a_ref, m_ref, *refs):
    d_refs = refs[:NX]
    near_ref, far_ref, id_ref, wide_ref, d_ref = refs[NX:]
    for s in range(NX):
        d_ref[(z_ref[NZ] + NX - s) % NX] = d_refs[s][...]
    row = iota((128, TOP * 128), 0) - META
    col = iota((128, TOP * 128), 1)
    q = col // 512
    k = col // 128 % 4
    block = col % 128 // FX
    origin = (block - k + 4) % 4
    j = 4 * q + jnp.where(origin == 1, 2, jnp.where(origin == 2, 1, origin))
    spread = jnp.dot(m_ref[...], (row == j).astype(F32).astype(BF), preferred_element_type=F32)
    tags = (spread - (iota((1, TOP * 128), 1) % 128 // FX).astype(F32)).astype(BF)
    for n in range(TOP):
        id_ref[n] = tags[:, n * 128 : (n + 1) * 128]

    def body(s, carry):
        r = pl.multiple_of(s * 16, 16)
        z = z_ref[s // 8]
        rr = pl.multiple_of((s % 8) * 16, 16)
        ids = [id_ref[n, pl.ds(r, 16), :] for n in range(TOP)]
        turned = []
        for n in range(2):
            a = a_ref[z, pl.ds(n * ZR + rr, 16), :].astype(F32)
            for shift in range(4):
                moved = a if shift == 0 else pltpu.roll(a, shift * FX, 1)
                turned.append(moved.astype(BF))
        for g in range(8):
            kept = jnp.zeros((16, 128), BF)
            for n in range(TOP):
                kept = jnp.where(ids[n] == jnp.asarray(4.0 * g, BF), turned[n], kept)
            wide_ref[g, pl.ds(r, 16), :] = kept
        return carry

    lax.fori_loop(0, ROWS // 16, body, 0, unroll=4)
    for x in range(NX):
        out = None
        for g in range(0, 8, 2):
            width = min(256, NE * FX - g * 128)
            wide = jnp.concatenate([wide_ref[g], wide_ref[g + 1]], axis=1)
            part = jnp.dot(
                wide[:, :width],
                d_ref[x, g * 128 : g * 128 + width],
                preferred_element_type=F32,
            )
            out = part if out is None else out + part
        out = out[:, :SLICE].astype(BF)
        near_ref[:, x * SLICE : (x + 1) * SLICE] = out[: ROWS // 2]
        far_ref[:, x * SLICE : (x + 1) * SLICE] = out[ROWS // 2 :]


def combine(blocks, acts, metas, down):
    return pl.pallas_call(
        combine_body,
        in_specs=[SMEM] + [VMEM] * (2 + NX),
        out_specs=[VMEM] * 2,
        out_shape=[jax.ShapeDtypeStruct((ROWS // 2, WIDE), BF)] * 2,
        scratch_shapes=[
            pltpu.VMEM((TOP, ROWS, 128), BF),
            pltpu.VMEM((8, ROWS, 128), BF),
            pltpu.VMEM((NX, NE * FX, GL), BF),
        ],
        compiler_params=pltpu.CompilerParams(vmem_limit_bytes=28 << 20),
        name="combine",
    )(blocks, acts, metas, *down)


def pack_body(h_ref, n_ref, e_ref, r_ref, l_ref, o_ref):
    widened = h_ref[...].astype(F32)
    scaled = (widened * n_ref[...].astype(F32)).astype(BF)
    squares = jnp.sum(widened * widened, axis=1, keepdims=True)
    high = squares.astype(BF).astype(F32)
    place = iota((RB, NE), 1)
    entries = [
        jnp.sum(
            jnp.where(l_ref[...] == e_ref[:, j : j + 1], place, 0), axis=1, keepdims=True
        ).astype(F32)
        for j in range(TOP)
    ]
    weight = r_ref[...]
    meta = entries + [
        (weight >> 6).astype(F32),
        (weight & 63).astype(F32),
        high,
        squares - high,
        jnp.zeros((RB, GL - SLICE - 26), F32),
    ]
    o_ref[...] = jnp.zeros((RB, NX * GL), BF)
    for k in range(NX):
        o_ref[:, k * GL : k * GL + SLICE] = scaled[:, k * SLICE : (k + 1) * SLICE]
    o_ref[:, SLICE:GL] = jnp.concatenate(meta, axis=1).astype(BF)


def pack_rows(hidden_in, norm_gain, expert_ids, route_weight, updated_list):
    return pl.pallas_call(
        pack_body,
        out_shape=jax.ShapeDtypeStruct((RB, NX * GL), BF),
        compiler_params=pltpu.CompilerParams(vmem_limit_bytes=4 << 20),
        name="pack_rows",
    )(hidden_in, norm_gain[None, :], expert_ids, route_weight, updated_list[None, :])


def gather_rows(packed):
    moved = swap_zt(packed)
    came = [shift_x(moved, s) for s in range(1, NX)]
    ring = jnp.concatenate([moved] + came, axis=0)
    mine = [ring] + [shift_y(ring, s) for s in range(1, NY)]
    return mine + [other_core(block) for block in mine]


def block_places():
    t = lax.axis_index("tensor")
    y, c = t // 2, t % 2
    s = jnp.arange(NY, dtype=jnp.int32)
    turn = (y - s) % NY * 2
    blocks = jnp.concatenate([turn + c, turn + 1 - c]).astype(jnp.int32)
    zs = jnp.arange(NZ, dtype=jnp.int32)
    places = (y - zs // 2) % NY + NY * (zs % 2 != c).astype(jnp.int32)
    return blocks, places.astype(jnp.int32)


def move_gate_up(pieces):
    ahead = shift_x(pieces[2], 1)
    behind = shift_x(pieces[4], NX - 1)
    came = [pieces[0], shift_x(pieces[1], 1), shift_x(pieces[3], NX - 1)]
    ahead = shift_x(ahead, 1)
    behind = shift_x(behind, NX - 1)
    return [came[0], came[1], ahead, came[2], behind]


def move_down(pieces):
    return [pieces[0]] + [shift_x(pieces[s], s) for s in range(1, NX)]


def place_body(own_ref, *refs):
    pieces, (out_ref,) = refs[:NX], refs[NX:]
    for s in range(NX):
        out_ref[:, (own_ref[0] + NX - s) % NX] = pieces[s][...]


def move_gate(chosen, own):
    came = lax.all_to_all(
        chosen.reshape(NZ, NX, SLICE, FT),
        "expert",
        split_axis=0,
        concat_axis=0,
        tiled=True,
        axis_index_groups=Z_GROUPS,
    )
    x = own[0]
    pieces = [
        lax.dynamic_index_in_dim(came, (x + s) % NX, 1, keepdims=False) for s in range(NX)
    ]
    pieces = [pieces[0]] + [shift_x(pieces[s], s) for s in range(1, NX)]
    return pl.pallas_call(
        place_body,
        in_specs=[SMEM] + [VMEM] * NX,
        out_specs=VMEM,
        out_shape=jax.ShapeDtypeStruct((NZ, NX, SLICE, FT), BF),
        compiler_params=pltpu.CompilerParams(vmem_limit_bytes=8 << 20),
        name="place_gate",
    )(own, *pieces).reshape(1, DIM, FT)


def add(values):
    total = values[0].astype(F32)
    for value in values[1:]:
        total = total + value.astype(F32)
    return total.astype(BF)


def gather_out(near, far):
    size = near.shape[0] // NY
    blocks = [
        add([near[s * size : (s + 1) * size], far[s * size : (s + 1) * size]]) for s in range(NY)
    ]
    came = [blocks[0]] + [shift_y(blocks[s], NY - s) for s in range(1, NY)]
    pieces = [add([b[s * RB : (s + 1) * RB] for b in came]) for s in range(NX)]
    came = [pieces[0]] + [shift_x(pieces[s], NX - s) for s in range(1, NX)]
    return swap_zt(add(came))


def device_body(
    query_latent,
    kv_cache,
    cache_len,
    value_up,
    hidden_in,
    norm_gain,
    expert_ids,
    route_weight,
    placement_plan,
    updated_list,
    learner_gate,
    learner_up,
    learner_down,
):
    own = (lax.axis_index("expert") % NX).astype(jnp.int32)[None]
    held = move_gate_up(turn_gate_up(own, learner_gate, learner_up))
    rows = gather_rows(pack_rows(hidden_in, norm_gain, expert_ids, route_weight, updated_list))
    blocks, places = block_places()
    blocks = jnp.concatenate([blocks, own])

    entry_range = jnp.arange(NE, dtype=jnp.int32)
    learner_entry = jnp.sum(
        entry_range[None, :] * (updated_list[None, :] == placement_plan[:, None]).astype(jnp.int32),
        axis=1,
    )
    slot_gate = move_gate(jnp.take(learner_gate, learner_entry, axis=0, mode="clip"), own)

    held_down = move_down(turn_down(own, learner_down))
    parts = exchange(project(blocks, rows, held), Z_GROUPS)
    z = lax.axis_index("expert") // NX
    metas = jnp.stack([block[:, 128:256] for block in rows])
    meta = lax.dynamic_index_in_dim(metas, places[z], 0, keepdims=False)
    acts = exchange(activate(parts, meta), Z_GROUPS)
    near, far = combine(blocks, acts, metas.reshape(ROWS, 128), held_down)
    far = other_core(far)
    moe_out = gather_out(near, far)

    latent = attend(query_latent, kv_cache, cache_len)
    head_rows = lax.all_to_all(latent, "tensor", split_axis=1, concat_axis=0, tiled=True)
    projected = jnp.einsum("rhc,hcv->rhv", head_rows, value_up, preferred_element_type=F32)
    attn_values = projected.astype(BF).reshape(
        head_rows.shape[0], projected.shape[1] * projected.shape[2]
    )
    return (attn_values, moe_out, slot_gate)


def solution(mesh):
    in_specs = (
        P(("expert", "tensor"), None, None),
        P(("expert", "tensor"), None, None),
        P(("expert", "tensor")),
        P("tensor", None, None),
        P("expert", "tensor"),
        P("tensor"),
        P("expert", None),
        P("expert", None),
        P(),
        P(),
        P(None, "expert", "tensor"),
        P(None, "expert", "tensor"),
        P(None, "expert", "tensor"),
    )
    out_specs = (P("expert", "tensor"), P("expert", "tensor"), P("expert", None, "tensor"))
    return jax.shard_map(
        device_body, mesh=mesh, in_specs=in_specs, out_specs=out_specs, check_vma=False
    )
```

```python
import jax
import jax.numpy as jnp
from jax import lax
from jax.experimental import pallas as pl
from jax.experimental.pallas import tpu as pltpu
from jax.sharding import PartitionSpec as P


KVL = 512
SCORE_SCALE = 192.0 ** (-0.5)
ROUTE_SCALE = 2.5
NORM_EPSILON = 1e-06

NZ, NX, NT, NY = 8, 4, 8, 4
RB = 32
ZR = NX * RB
ROWS = NZ * ZR
SLICE = 224
WIDE = NX * SLICE
GL = 256
FT = 128
FX = FT // NX
NE = 30
TOP = 8
DIM = 7168

Z_GROUPS = [[z * NX + x for z in range(NZ)] for x in range(NX)]
SWAP = [
    ((z * NX + x) * NT + t, (t * NX + x) * NT + z)
    for z in range(NZ)
    for x in range(NX)
    for t in range(NT)
]
BF = jnp.bfloat16
F32 = jnp.float32


def swap_zt(value):
    return lax.ppermute(value, ("expert", "tensor"), SWAP)


def exchange(value, groups):
    return lax.all_to_all(
        value, "expert", split_axis=0, concat_axis=0, tiled=True, axis_index_groups=groups
    )


def shift_x(value, step):
    pairs = [(z * NX + x, z * NX + (x + step) % NX) for z in range(NZ) for x in range(NX)]
    return lax.ppermute(value, "expert", pairs)


def shift_y(value, step):
    pairs = [(y * 2 + c, (y + step) % NY * 2 + c) for y in range(NY) for c in range(2)]
    return lax.ppermute(value, "tensor", pairs)


def other_core(value):
    return lax.ppermute(value, "tensor", [(t, t ^ 1) for t in range(NT)])


def attend(query_latent, kv_cache, cache_len):
    scores = (
        jnp.einsum("rhc,rpc->rhp", query_latent, kv_cache, preferred_element_type=F32)
        * SCORE_SCALE
    )
    allowed = (jnp.arange(kv_cache.shape[1], dtype=jnp.int32)[None, :] < cache_len[:, None])[
        :, None, :
    ]
    scores = jnp.where(allowed, scores, -1e30)
    highest = jnp.max(scores, axis=2, keepdims=True)
    lifted = jnp.where(allowed, jnp.exp(scores - highest), 0.0)
    totals = jnp.sum(lifted, axis=2, keepdims=True)
    mixed = jnp.einsum(
        "rhp,rpc->rhc",
        lifted.astype(BF),
        kv_cache[:, :, :KVL],
        preferred_element_type=F32,
    )
    return (mixed / totals).astype(BF)


def iota(shape, axis):
    return lax.broadcasted_iota(jnp.int32, shape, axis)


def flip(block):
    turned = jnp.transpose(block.astype(F32))
    return jnp.concatenate([turned, jnp.zeros((FT, GL - SLICE), F32)], axis=1).astype(BF)


SMEM = pl.BlockSpec(memory_space=pltpu.SMEM)
VMEM = pl.BlockSpec(memory_space=pltpu.VMEM)
HEAD = 16


def gate_up_body(own_ref, g_ref, u_ref, *refs):
    outs, (turn_ref,) = refs[:5], refs[5:]
    own = own_ref[0]

    def turn(e, carry):
        turn_ref[0, e] = flip(g_ref[e])
        turn_ref[1, e] = flip(u_ref[e])
        return carry

    lax.fori_loop(0, NE, turn, 0, unroll=5)
    for s in range(NX):
        at = pl.multiple_of((own + s) % NX * FX, FX)
        spans = [(outs[s], 0, NE)]
        if s == 2:
            spans = [(outs[2], 0, HEAD), (outs[4], HEAD, NE)]
        for out, low, high in spans:

            def copy(e, carry, out=out, low=low, at=at):
                row = pl.multiple_of((e - low) * 2 * FX, 2 * FX)
                out[pl.ds(row, FX)] = turn_ref[0, e, pl.ds(at, FX), :]
                out[pl.ds(row + FX, FX)] = turn_ref[1, e, pl.ds(at, FX), :]
                return carry

            lax.fori_loop(low, high, copy, 0, unroll=2)


def down_body(own_ref, d_ref, *refs):
    outs, (turn_ref,) = refs[:NX], refs[NX:]
    own = own_ref[0]

    def turn(e, carry):
        turn_ref[e] = flip(d_ref[e])
        return carry

    lax.fori_loop(0, NE, turn, 0, unroll=5)
    for s in range(NX):
        at = pl.multiple_of((own + s) % NX * FX, FX)

        def copy(e, carry, out=outs[s], at=at):
            row = pl.multiple_of(e * FX, FX)
            out[pl.ds(row, FX)] = turn_ref[e, pl.ds(at, FX), :]
            return carry

        lax.fori_loop(0, NE, copy, 0, unroll=3)


def turn_gate_up(own, gate, up):
    sizes = [NE, NE, HEAD, NE, NE - HEAD]
    return pl.pallas_call(
        gate_up_body,
        in_specs=[SMEM, VMEM, VMEM],
        out_specs=[VMEM] * 5,
        out_shape=[jax.ShapeDtypeStruct((n * 2 * FX, GL), BF) for n in sizes],
        scratch_shapes=[pltpu.VMEM((2, NE, FT, GL), BF)],
        compiler_params=pltpu.CompilerParams(vmem_limit_bytes=20 << 20),
        name="turn_gate_up",
    )(own, gate, up)


def turn_down(own, down):
    return pl.pallas_call(
        down_body,
        in_specs=[SMEM, VMEM],
        out_specs=[VMEM] * NX,
        out_shape=[jax.ShapeDtypeStruct((NE * FX, GL), BF)] * NX,
        scratch_shapes=[pltpu.VMEM((NE, FT, GL), BF)],
        compiler_params=pltpu.CompilerParams(vmem_limit_bytes=14 << 20),
        name="turn_down",
    )(own, down)


META = 96
HIGH, LOW, SQ = META + 8, META + 16, META + 24
PR = 4 * ZR
PB = PR + 16


def project_body(z_ref, *refs):
    x_refs, w_refs = refs[:NZ], refs[NZ : NZ + 5]
    p_ref, m_ref, id_ref, y_ref = refs[NZ + 5 :]
    for n in range(NZ):
        m_ref[z_ref[n]] = x_refs[n][:, 128:256]
    meta = jnp.concatenate([x[:, 128:256] for x in x_refs], axis=0)
    col = iota((128, TOP * 128), 1)
    pick = (iota((128, TOP * 128), 0) - META == col // 128).astype(F32).astype(BF)
    spread = jnp.dot(meta, pick, preferred_element_type=F32)
    half = (iota((1, TOP * 128), 1) % 128 // 64).astype(F32)
    tags = (spread - half).astype(BF)
    for j in range(TOP):
        id_ref[j] = tags[:, j * 128 : (j + 1) * 128]
    xs = []
    for s in range(NX):
        lane = pl.multiple_of((z_ref[NZ] + NX - s) % NX * GL, GL)
        xs.append(jnp.concatenate([x[:, pl.ds(lane, GL)] for x in x_refs], axis=0))
    for start in range(0, NE * 2 * FX, 256):
        size = min(256, NE * 2 * FX - start)
        total = None
        for s in range(NX):
            w_ref, row = w_refs[s], start
            if s == 2 and start >= HEAD * 2 * FX:
                w_ref, row = w_refs[4], start - HEAD * 2 * FX
            part = lax.dot_general(
                xs[s],
                w_ref[row : row + size, :],
                (((1,), (1,)), ((), ())),
                preferred_element_type=F32,
            )
            total = part if total is None else total + part
        total = total.astype(BF)
        for n in range(size // 128):
            y_ref[start // 128 + n] = total[:, n * 128 : (n + 1) * 128]
    low_half = iota((16, 128), 1) < 64

    def body(s, carry):
        r = pl.multiple_of(s * 16, 16)
        z = z_ref[s // 8]
        rr = pl.multiple_of((s % 8) * 16, 16)
        ids = [id_ref[j, pl.ds(r, 16), :] for j in range(TOP)]
        kept = [jnp.zeros((16, 128), BF) for _ in range(TOP)]
        for tile in range(NE // 2):
            y = y_ref[tile, pl.ds(r, 16), :]
            for j in range(TOP):
                kept[j] = jnp.where(ids[j] == jnp.asarray(2.0 * tile, BF), y, kept[j])
        for q in range(TOP // 2):
            a = kept[2 * q].astype(F32)
            b = kept[2 * q + 1].astype(F32)
            a = a + pltpu.roll(a, 64, 1)
            b = b + pltpu.roll(b, 64, 1)
            p_ref[z, pl.ds(q * ZR + rr, 16), :] = jnp.where(low_half, a, b).astype(BF)
        return carry

    lax.fori_loop(0, ROWS // 16, body, 0, unroll=4)
    for n in range(NZ):
        turned = jnp.transpose(x_refs[n][:, 128:256].astype(F32))
        p_ref[z_ref[n], PR:PB, :] = turned[112:128].astype(BF)


def project(blocks, rows, weights):
    return pl.pallas_call(
        project_body,
        in_specs=[SMEM] + [VMEM] * (NZ + 5),
        out_specs=[VMEM] * 2,
        out_shape=[
            jax.ShapeDtypeStruct((NZ, PB, 128), BF),
            jax.ShapeDtypeStruct((NZ, ZR, 128), BF),
        ],
        scratch_shapes=[
            pltpu.VMEM((TOP, ROWS, 128), BF),
            pltpu.VMEM((NE // 2, ROWS, 128), BF),
        ],
        compiler_params=pltpu.CompilerParams(vmem_limit_bytes=32 << 20),
        name="project",
    )(blocks, *rows, *weights)


def activate_body(z_ref, p_ref, m_ref, o_ref):
    row = iota((128, 5 * 128), 0)
    col = iota((128, 5 * 128), 1)
    j = 2 * (col // 128) + (col % 128) // 64
    single = jnp.where(row == HIGH + j, 64.0, jnp.where(row == LOW + j, 1.0, 0.0))
    every = jnp.where(
        (row >= HIGH) & (row < LOW), 64.0, jnp.where((row >= LOW) & (row < SQ), 1.0, 0.0)
    )
    pick = jnp.where(col < 512, single, every).astype(BF)
    weights = jnp.dot(m_ref[z_ref[0]], pick, preferred_element_type=F32)
    scale = ROUTE_SCALE / weights[:, 512:640]
    squares = jnp.zeros((16, 128), F32)
    for z in range(NZ):
        squares = squares + p_ref[z, PR:PB, :].astype(F32)
    total = squares[8:9] + squares[9:10]
    inv = lax.rsqrt(total * (1.0 / DIM) + NORM_EPSILON)
    inv = jnp.transpose(jnp.broadcast_to(inv, (128, 128)))
    acts = []
    for q in range(TOP // 2):
        v = jnp.zeros((ZR, 128), F32)
        for z in range(NZ):
            v = v + p_ref[z, q * ZR : (q + 1) * ZR, :].astype(F32)
        v = v * inv
        u = pltpu.roll(v, 128 - FX, 1)
        gate = weights[:, q * 128 : (q + 1) * 128] * scale
        acts.append(v / (1.0 + jnp.exp(-v)) * u * gate)
    first = iota((ZR, 128), 1) % 64 < FX
    for q in range(2):
        packed = jnp.where(first, acts[2 * q], pltpu.roll(acts[2 * q + 1], FX, 1)).astype(BF)
        for z in range(NZ):
            o_ref[z, q * ZR : (q + 1) * ZR, :] = packed


def activate(z, parts, metas):
    return pl.pallas_call(
        activate_body,
        in_specs=[SMEM] + [VMEM] * 2,
        out_shape=jax.ShapeDtypeStruct((NZ, 2 * ZR, 128), BF),
        compiler_params=pltpu.CompilerParams(vmem_limit_bytes=12 << 20),
        name="activate",
    )(z, parts, metas)


def combine_body(z_ref, a_ref, m_ref, *refs):
    d_refs = refs[:NX]
    near_ref, far_ref, id_ref, wide_ref, d_ref = refs[NX:]
    for s in range(NX):
        d_ref[(z_ref[NZ] + NX - s) % NX] = d_refs[s][...]
    row = iota((128, TOP * 128), 0) - META
    col = iota((128, TOP * 128), 1)
    q = col // 512
    k = col // 128 % 4
    block = col % 128 // FX
    origin = (block - k + 4) % 4
    j = 4 * q + jnp.where(origin == 1, 2, jnp.where(origin == 2, 1, origin))
    meta = jnp.concatenate([m_ref[z_ref[n]] for n in range(NZ)], axis=0)
    spread = jnp.dot(meta, (row == j).astype(F32).astype(BF), preferred_element_type=F32)
    tags = (spread - (iota((1, TOP * 128), 1) % 128 // FX).astype(F32)).astype(BF)
    for n in range(TOP):
        id_ref[n] = tags[:, n * 128 : (n + 1) * 128]

    def body(s, carry):
        r = pl.multiple_of(s * 16, 16)
        z = z_ref[s // 8]
        rr = pl.multiple_of((s % 8) * 16, 16)
        ids = [id_ref[n, pl.ds(r, 16), :] for n in range(TOP)]
        turned = []
        for n in range(2):
            a = a_ref[z, pl.ds(n * ZR + rr, 16), :].astype(F32)
            for shift in range(4):
                moved = a if shift == 0 else pltpu.roll(a, shift * FX, 1)
                turned.append(moved.astype(BF))
        for g in range(8):
            kept = jnp.zeros((16, 128), BF)
            for n in range(TOP):
                kept = jnp.where(ids[n] == jnp.asarray(4.0 * g, BF), turned[n], kept)
            wide_ref[g, pl.ds(r, 16), :] = kept
        return carry

    lax.fori_loop(0, ROWS // 16, body, 0, unroll=4)
    for x in range(NX):
        out = None
        for g in range(0, 8, 2):
            width = min(256, NE * FX - g * 128)
            wide = jnp.concatenate([wide_ref[g], wide_ref[g + 1]], axis=1)
            part = jnp.dot(
                wide[:, :width],
                d_ref[x, g * 128 : g * 128 + width],
                preferred_element_type=F32,
            )
            out = part if out is None else out + part
        out = out[:, :SLICE].astype(BF)
        near_ref[:, x * SLICE : (x + 1) * SLICE] = out[: ROWS // 2]
        far_ref[:, x * SLICE : (x + 1) * SLICE] = out[ROWS // 2 :]


def combine(blocks, acts, metas, down):
    return pl.pallas_call(
        combine_body,
        in_specs=[SMEM] + [VMEM] * (2 + NX),
        out_specs=[VMEM] * 2,
        out_shape=[jax.ShapeDtypeStruct((ROWS // 2, WIDE), BF)] * 2,
        scratch_shapes=[
            pltpu.VMEM((TOP, ROWS, 128), BF),
            pltpu.VMEM((8, ROWS, 128), BF),
            pltpu.VMEM((NX, NE * FX, GL), BF),
        ],
        compiler_params=pltpu.CompilerParams(vmem_limit_bytes=28 << 20),
        name="combine",
    )(blocks, acts, metas, *down)


def pack_body(h_ref, n_ref, e_ref, r_ref, l_ref, o_ref):
    widened = h_ref[...].astype(F32)
    scaled = (widened * n_ref[...].astype(F32)).astype(BF)
    squares = jnp.sum(widened * widened, axis=1, keepdims=True)
    high = squares.astype(BF).astype(F32)
    place = iota((RB, NE), 1)
    entries = [
        jnp.sum(
            jnp.where(l_ref[...] == e_ref[:, j : j + 1], place, 0), axis=1, keepdims=True
        ).astype(F32)
        for j in range(TOP)
    ]
    weight = r_ref[...]
    meta = entries + [
        (weight >> 6).astype(F32),
        (weight & 63).astype(F32),
        high,
        squares - high,
        jnp.zeros((RB, GL - SLICE - 26), F32),
    ]
    o_ref[...] = jnp.zeros((RB, NX * GL), BF)
    for k in range(NX):
        o_ref[:, k * GL : k * GL + SLICE] = scaled[:, k * SLICE : (k + 1) * SLICE]
    o_ref[:, SLICE:GL] = jnp.concatenate(meta, axis=1).astype(BF)


def pack_rows(hidden_in, norm_gain, expert_ids, route_weight, updated_list):
    return pl.pallas_call(
        pack_body,
        out_shape=jax.ShapeDtypeStruct((RB, NX * GL), BF),
        compiler_params=pltpu.CompilerParams(vmem_limit_bytes=4 << 20),
        name="pack_rows",
    )(hidden_in, norm_gain[None, :], expert_ids, route_weight, updated_list[None, :])


def gather_rows(packed):
    moved = swap_zt(packed)
    came = [shift_x(moved, s) for s in range(1, NX)]
    ring = jnp.concatenate([moved] + came, axis=0)
    mine = [ring] + [shift_y(ring, s) for s in range(1, NY)]
    return mine + [other_core(block) for block in mine]


def block_places():
    t = lax.axis_index("tensor").astype(jnp.int32)
    n = jnp.arange(NZ, dtype=jnp.int32)
    return ((t // 2 + NY - n % NY) % NY) * 2 + (t + n // NY) % 2


def move_gate_up(pieces):
    ahead = shift_x(pieces[2], 1)
    behind = shift_x(pieces[4], NX - 1)
    came = [pieces[0], shift_x(pieces[1], 1), shift_x(pieces[3], NX - 1)]
    ahead = shift_x(ahead, 1)
    behind = shift_x(behind, NX - 1)
    return [came[0], came[1], ahead, came[2], behind]


def move_down(pieces):
    return [pieces[0]] + [shift_x(pieces[s], s) for s in range(1, NX)]


def place_body(own_ref, *refs):
    pieces, (out_ref,) = refs[:NX], refs[NX:]
    for s in range(NX):
        out_ref[:, (own_ref[0] + NX - s) % NX] = pieces[s][...]


def move_gate(chosen, own):
    came = lax.all_to_all(
        chosen.reshape(NZ, NX, SLICE, FT),
        "expert",
        split_axis=0,
        concat_axis=0,
        tiled=True,
        axis_index_groups=Z_GROUPS,
    )
    x = own[0]
    pieces = [
        lax.dynamic_index_in_dim(came, (x + s) % NX, 1, keepdims=False) for s in range(NX)
    ]
    pieces = [pieces[0]] + [shift_x(pieces[s], s) for s in range(1, NX)]
    return pl.pallas_call(
        place_body,
        in_specs=[SMEM] + [VMEM] * NX,
        out_specs=VMEM,
        out_shape=jax.ShapeDtypeStruct((NZ, NX, SLICE, FT), BF),
        compiler_params=pltpu.CompilerParams(vmem_limit_bytes=8 << 20),
        name="place_gate",
    )(own, *pieces).reshape(1, DIM, FT)


def add(values):
    total = values[0].astype(F32)
    for value in values[1:]:
        total = total + value.astype(F32)
    return total.astype(BF)


def gather_out(near, far):
    size = near.shape[0] // NY
    blocks = [
        add([near[s * size : (s + 1) * size], far[s * size : (s + 1) * size]]) for s in range(NY)
    ]
    came = [blocks[0]] + [shift_y(blocks[s], NY - s) for s in range(1, NY)]
    pieces = [add([b[s * RB : (s + 1) * RB] for b in came]) for s in range(NX)]
    came = [pieces[0]] + [shift_x(pieces[s], NX - s) for s in range(1, NX)]
    return swap_zt(add(came))


def device_body(
    query_latent,
    kv_cache,
    cache_len,
    value_up,
    hidden_in,
    norm_gain,
    expert_ids,
    route_weight,
    placement_plan,
    updated_list,
    learner_gate,
    learner_up,
    learner_down,
):
    own = (lax.axis_index("expert") % NX).astype(jnp.int32)[None]
    held = move_gate_up(turn_gate_up(own, learner_gate, learner_up))
    rows = gather_rows(pack_rows(hidden_in, norm_gain, expert_ids, route_weight, updated_list))
    blocks = jnp.concatenate([block_places(), own])

    entry_range = jnp.arange(NE, dtype=jnp.int32)
    learner_entry = jnp.sum(
        entry_range[None, :] * (updated_list[None, :] == placement_plan[:, None]).astype(jnp.int32),
        axis=1,
    )
    slot_gate = move_gate(jnp.take(learner_gate, learner_entry, axis=0, mode="clip"), own)

    held_down = move_down(turn_down(own, learner_down))
    sums, metas = project(blocks, rows, held)
    parts = exchange(sums, Z_GROUPS)
    z = (lax.axis_index("expert") // NX).astype(jnp.int32)[None]
    acts = exchange(activate(z, parts, metas), Z_GROUPS)
    near, far = combine(blocks, acts, metas, held_down)
    far = other_core(far)
    moe_out = gather_out(near, far)

    latent = attend(query_latent, kv_cache, cache_len)
    head_rows = lax.all_to_all(latent, "tensor", split_axis=1, concat_axis=0, tiled=True)
    projected = jnp.einsum("rhc,hcv->rhv", head_rows, value_up, preferred_element_type=F32)
    attn_values = projected.astype(BF).reshape(
        head_rows.shape[0], projected.shape[1] * projected.shape[2]
    )
    return (attn_values, moe_out, slot_gate)


def solution(mesh):
    in_specs = (
        P(("expert", "tensor"), None, None),
        P(("expert", "tensor"), None, None),
        P(("expert", "tensor")),
        P("tensor", None, None),
        P("expert", "tensor"),
        P("tensor"),
        P("expert", None),
        P("expert", None),
        P(),
        P(),
        P(None, "expert", "tensor"),
        P(None, "expert", "tensor"),
        P(None, "expert", "tensor"),
    )
    out_specs = (P("expert", "tensor"), P("expert", "tensor"), P("expert", None, "tensor"))
    return jax.shard_map(
        device_body, mesh=mesh, in_specs=in_specs, out_specs=out_specs, check_vma=False
    )
```
